32 devices in a mesh: dp: 4 (over y, x), ctx: 8 (over z, core).
Axes of the slice: x: 2, y: 2, z: 4, core: 2. Of those that a mesh axis runs over, the one named last changes fastest.
Arguments:
- inputs: bfloat16 [8192, 896], P(('dp', 'ctx')), may hold values from -6 to 6
- cotangent: bfloat16 [8192, 896], P(('dp', 'ctx')), may hold values from -6 to 6
- parents: int32 [4, 9], P('dp'), may hold values from 0 to 7, as said below
- lengths: int32 [4, 9], P('dp'), may hold values from 64 to 1408, as said below
- positions: int32 [8192], P(('dp', 'ctx')), may hold values from 0 to 2047, as said below
- master: float32 [116512, 128], P(('dp', 'ctx'))
- moment_one: float32 [116512, 128], P(('dp', 'ctx')), may hold values from -0.6 to 0.6
- moment_two: float32 [116512, 128], P(('dp', 'ctx')), may hold values from 0.005 to 0.05
Outputs:
- activations: bfloat16 [8192, 896], P(('dp', 'ctx'))
- input_grad: float32 [8192, 896], P(('dp', 'ctx'))
- new_master: float32 [116512, 128], P(('dp', 'ctx'))
- new_moment_one: float32 [116512, 128], P(('dp', 'ctx'))
- new_moment_two: float32 [116512, 128], P(('dp', 'ctx'))
The draws below stay inside these ranges and needn't reach their ends.
Inputs may be any that keep to these rules, and one draw needn't show every extreme that they name: parents[b, 0] = 0 (segment 0 is the trunk) and parents[b, s] < s for s >= 1, so a segment's ancestors come before it; in tree 0 the segments form one chain, parents[0, s] = s - 1. `lengths`: each row sums to 2048; segments other than the trunk hold 64 to 192 tokens; in tree 0 all of them hold 64 tokens but one, which holds 192. `positions`: a token's position is its offset within its segment plus the lengths of all strict ancestors of its segment.
All inputs are finite; a program needn't handle non-finite values.
Results may differ from the reference program's by a relative error of at most 0.012.
Values may be sent and summed in bfloat16 or wider, within the bound.
No kernel may reach another device: no remote copies, remote signals or barrier semaphores. Data moves between devices by JAX's collectives and lax.ppermute only.
A program may use at most 384 MiB of HBM per device.

```python
import math
import jax
import jax.numpy as jnp
from jax import lax

D = 896
HEADS = 14
KV_HEADS = 2
HEAD = 64
FF = 4864
TREE_LEN = 2048
BRANCH = 128
SEGS = 9
STEP = 10
TOKENS = 8192
TREES = 4
ROWS = 116512


def tree_tables(key):
    base_key = jax.random.fold_in(key, 17)
    par_key, len_key, pick_key, other_key = jax.random.split(base_key, 4)
    seg_iota = jnp.arange(SEGS, dtype=jnp.int32)
    tree_iota = jnp.arange(TREES, dtype=jnp.int32)[:, None]
    raw_parent = jax.random.randint(par_key, (TREES, SEGS), 0, 1 << 20, dtype=jnp.int32)
    parents = (raw_parent % jnp.maximum(seg_iota, 1)[None, :]).astype(jnp.int32)
    chain_parent = jnp.maximum(seg_iota - 1, 0)[None, :]
    parents = jnp.where(tree_iota == 0, chain_parent, parents).astype(jnp.int32)
    shortest = BRANCH // 2
    longest = 3 * BRANCH // 2
    branch_len = jax.random.randint(len_key, (TREES, SEGS - 1), shortest, longest + 1, dtype=jnp.int32)
    branch_len = jnp.where(tree_iota == 0, shortest, branch_len)
    first_col = jax.random.randint(pick_key, (TREES, 1), 0, SEGS - 1, dtype=jnp.int32)
    shift_col = jax.random.randint(other_key, (TREES, 1), 1, SEGS - 1, dtype=jnp.int32)
    second_col = (first_col + shift_col) % (SEGS - 1)
    col_iota = jnp.arange(SEGS - 1, dtype=jnp.int32)[None, :]
    branch_len = jnp.where(col_iota == first_col, shortest, branch_len)
    branch_len = jnp.where(col_iota == second_col, longest, branch_len)
    trunk_len = TREE_LEN - jnp.sum(branch_len, axis=1, keepdims=True)
    lengths = jnp.concatenate([trunk_len, branch_len], axis=1).astype(jnp.int32)
    ancestor_len = jnp.zeros((TREES, SEGS), jnp.int32)
    current = jnp.broadcast_to(seg_iota[None, :], (TREES, SEGS))
    for repeat_idx in range(SEGS):
        parent_of = jnp.take_along_axis(parents, current, axis=1)
        ancestor_len = ancestor_len + jnp.where(current > 0, jnp.take_along_axis(lengths, parent_of, axis=1), 0)
        current = jnp.where(current > 0, parent_of, 0)
    seg_ends = jnp.cumsum(lengths, axis=1).astype(jnp.int32)
    token_iota = jnp.arange(TREE_LEN, dtype=jnp.int32)
    seg_ids = jnp.sum((token_iota[None, :, None] >= seg_ends[:, None, :]).astype(jnp.int32), axis=2)
    starts = jnp.take_along_axis(seg_ends - lengths, seg_ids, axis=1)
    depth_len = jnp.take_along_axis(ancestor_len, seg_ids, axis=1)
    positions = (token_iota[None, :] - starts + depth_len).reshape(TREES * TREE_LEN)
    return (parents, lengths, positions.astype(jnp.int32))


def draw_parents(key, part):
    return tree_tables(key)[0]


def draw_lengths(key, part):
    return tree_tables(key)[1]


def draw_positions(key, part):
    return tree_tables(key)[2]


def draw_master(key, part):
    q_width = HEADS * HEAD
    kv_width = KV_HEADS * HEAD
    amounts = [D * q_width, q_width, D * kv_width, kv_width, D * kv_width, kv_width, q_width * D, D * FF, D * FF, FF * D, D, D]
    factors = [D ** (-0.5), 0.3, D ** (-0.5), 0.3, D ** (-0.5), 0.3, 6.0 * q_width ** (-0.5), D ** (-0.5), D ** (-0.5), FF ** (-0.5), 0.0, 0.0]
    total_len = ROWS * 128
    flat_iota = jnp.arange(total_len)
    normal_vals = jnp.clip(jax.random.normal(jax.random.fold_in(key, 3), (total_len,), jnp.float32), -4.0, 4.0)
    scale_vec = jnp.zeros((total_len,), jnp.float32)
    offset = 0
    for amount, factor in zip(amounts, factors):
        inside = (flat_iota >= offset) & (flat_iota < offset + amount)
        scale_vec = jnp.where(inside, factor, scale_vec)
        offset += amount
    gain_mask = (flat_iota >= offset - 2 * D) & (flat_iota < offset)
    values = jnp.where(gain_mask, 1.0 + 0.1 * normal_vals, normal_vals * scale_vec)
    return values.reshape(ROWS, 128).astype(jnp.float32)


def block_levels(own_key, shape, cuts, least, top_value):
    factor_of, own = 1.0, jax.random.fold_in(own_key, 6)
    for dim, blocks in cuts:
        draws = jnp.exp(jax.random.uniform(jax.random.fold_in(own, dim), (blocks,), jnp.float32, least / len(cuts), top_value / len(cuts)))
        factor_of = factor_of * jnp.repeat(draws, shape[dim] // blocks).reshape([-1 if axis == dim else 1 for axis in range(len(shape))])
    return factor_of


def centred(rng, extent, deviation, bound, cuts=(), kind=jnp.bfloat16):
    result = deviation * jax.random.normal(rng, extent, jnp.float32)
    if cuts:
        result = result * block_levels(rng, extent, cuts, -0.22, 0.18)
    return jnp.clip(result, -bound, bound).astype(kind)


def setup_inputs(seed: int = 0) -> dict:
    streams_of = jax.random.split(jax.random.key(seed), 9)
    inputs = centred(streams_of[0], (TOKENS, D), 1.0, 6.0, ((0, 32),))
    cotangent = centred(streams_of[1], (TOKENS, D), 1.0, 6.0, ((0, 32),))
    parents = draw_parents(jax.random.fold_in(streams_of[8], 71), 0)
    lengths = draw_lengths(jax.random.fold_in(streams_of[8], 71), 0)
    positions = draw_positions(jax.random.fold_in(streams_of[8], 71), 0)
    master = draw_master(jax.random.fold_in(streams_of[8], 71), 0)
    moment_one = centred(streams_of[6], (ROWS, 128), 0.1, 0.6, ((0, 32),), jnp.float32)
    moment_two = jnp.clip(jnp.exp(math.log(0.05) - 2.3025851 * jax.random.uniform(streams_of[7], (ROWS, 128), jnp.float32) ** block_levels(streams_of[7], (ROWS, 128), ((0, 32),), -0.2, 0.2)), 0.005, 0.05)
    return {"inputs": inputs, "cotangent": cotangent, "parents": parents, "lengths": lengths, "positions": positions, "master": master, "moment_one": moment_one, "moment_two": moment_two}


RMS_EPS = 1e-06
ROPE_BASE = 1000000.0
BETA_ONE = 0.9
BETA_TWO = 0.95
ADAM_EPS = 1e-08
LEARN_RATE = 0.01
DECAY_RATE = 0.1
NEG_FILL = -1e+30

@jax.custom_vjp
def low(v):
    return lax.optimization_barrier(v.astype(jnp.bfloat16)).astype(jnp.float32)

@jax.custom_vjp
def low_back(v):
    return v

def low_keep(v):
    return (low(v), None)

def low_pass(kept, grad):
    return (grad,)

def back_keep(v):
    return (v, None)

def back_low(kept, grad):
    return (low(grad),)
low.defvjp(low_keep, low_pass)
low_back.defvjp(back_keep, back_low)

def param_shapes():
    q_width = HEADS * HEAD
    kv_width = KV_HEADS * HEAD
    return [(D, q_width), (q_width,), (D, kv_width), (kv_width,), (D, kv_width), (kv_width,), (q_width, D), (D, FF), (D, FF), (FF, D), (D,), (D,)]

def unpack(flat_vec):
    pieces = []
    offset = 0
    for dims in param_shapes():
        amount = math.prod(dims)
        pieces.append(flat_vec[offset:offset + amount].reshape(dims))
        offset += amount
    return pieces

def exact_dot(left_mat, right_mat):
    return jnp.dot(left_mat, right_mat, precision=lax.Precision.HIGHEST, preferred_element_type=jnp.float32)

def rms_scale(values):
    return lax.rsqrt(lax.optimization_barrier(jnp.mean(values * values, axis=-1, keepdims=True)) + RMS_EPS)

def rotate(values, positions):
    half_dim = HEAD // 2
    inverse = ROPE_BASE ** (-(jnp.arange(half_dim, dtype=jnp.float32) * 2.0 / HEAD))
    angles = positions.astype(jnp.float32)[:, None] * inverse[None, :]
    cosine = jnp.cos(angles)[:, None, :]
    sine_vals = jnp.sin(angles)[:, None, :]
    first_half = values[..., :half_dim]
    second_half = values[..., half_dim:]
    return jnp.concatenate([first_half * cosine - second_half * sine_vals, second_half * cosine + first_half * sine_vals], axis=-1)

def ancestry_matrix(parent_row):
    seg_iota = jnp.arange(SEGS)
    parent_step_matrix = ((parent_row[:, None] == seg_iota[None, :]) & (seg_iota[:, None] > 0)).astype(jnp.float32)
    identity_matrix = jnp.eye(SEGS, dtype=jnp.float32)
    reachable_mask = identity_matrix
    for repeat_idx in range(SEGS):
        reachable_mask = jnp.minimum(identity_matrix + exact_dot(parent_step_matrix, reachable_mask), 1.0)
    return reachable_mask

def forward(weight_list, inputs, visible, positions):
    w_query, b_query, w_key, b_key, w_value, b_value, w_out, w_gate, w_up, w_down, norm_one, norm_two = weight_list
    length = inputs.shape[0]
    groups = HEADS // KV_HEADS
    normed = low(inputs * rms_scale(inputs) * norm_one)
    query_rot = low(rotate(low_back(exact_dot(normed, w_query) + b_query).reshape(length, HEADS, HEAD), positions))
    key_rot = low(rotate(low_back(exact_dot(normed, w_key) + b_key).reshape(length, KV_HEADS, HEAD), positions))
    value_vec = low(low_back(exact_dot(normed, w_value) + b_value)).reshape(length, KV_HEADS, HEAD)
    query_rot = query_rot.reshape(length, KV_HEADS, groups, HEAD)
    scores = jnp.einsum('qkgd,nkd->kgqn', query_rot, key_rot, precision=lax.Precision.HIGHEST) * HEAD ** (-0.5)
    scores = jnp.where(visible[None, None], low_back(scores), NEG_FILL)
    attn_probs = low(jax.nn.softmax(scores, axis=-1))
    attended = jnp.einsum('kgqn,nkd->qkgd', attn_probs, value_vec, precision=lax.Precision.HIGHEST).reshape(length, HEADS * HEAD)
    branch = low_back(exact_dot(low(low_back(attended)), w_out))
    midway_hidden = inputs + branch
    second = low(midway_hidden * rms_scale(midway_hidden) * norm_two)
    gate_act = low_back(exact_dot(second, w_gate))
    up_act = low_back(exact_dot(second, w_up))
    hidden = low(jax.nn.silu(gate_act) * up_act)
    return midway_hidden + low_back(exact_dot(hidden, w_down))

def reference(inputs, cotangent, parents, lengths, positions, master, moment_one, moment_two):
    weight_list = unpack(master.astype(jnp.bfloat16).astype(jnp.float32).reshape(-1))
    tree_count = parents.shape[0]
    token_iota = jnp.arange(TREE_LEN)
    used_count = sum((math.prod(dims) for dims in param_shapes()))

    def per_tree(grad_total, tree_items):
        tree_in, tree_cot, tree_par, tree_len, tree_pos = tree_items
        reachable_mask = ancestry_matrix(tree_par)
        seg_ends = jnp.cumsum(tree_len)
        seg_ids = lax.optimization_barrier(jnp.sum((token_iota[:, None] >= seg_ends[None, :]).astype(jnp.int32), axis=1)).astype(jnp.int32)
        visible = (reachable_mask[seg_ids[:, None], seg_ids[None, :]] > 0.5) & (token_iota[None, :] <= token_iota[:, None])

        def tree_fn(weights_in, tree_x):
            return forward(weights_in, tree_x, visible, tree_pos)
        outputs, pullback = jax.vjp(tree_fn, weight_list, tree_in.astype(jnp.float32))
        grad_w, grad_x = pullback(tree_cot.astype(jnp.float32))
        flat_grad = jnp.concatenate([grad_piece.reshape(-1) for grad_piece in grad_w])
        return (grad_total + flat_grad, (outputs.astype(jnp.bfloat16), grad_x))
    scan_items = (inputs.reshape(tree_count, TREE_LEN, D), cotangent.reshape(tree_count, TREE_LEN, D), parents, lengths, positions.reshape(tree_count, TREE_LEN))
    grad_total, (outputs, grad_inputs) = lax.scan(per_tree, jnp.zeros((used_count,), jnp.float32), scan_items)
    padded = jnp.pad(grad_total, (0, master.size - used_count)).reshape(master.shape) * TOKENS ** (-0.5)
    new_one = BETA_ONE * moment_one + (1.0 - BETA_ONE) * padded
    new_two = BETA_TWO * moment_two + (1.0 - BETA_TWO) * padded * padded
    corrected_one = new_one / (1.0 - BETA_ONE ** STEP)
    corrected_two = new_two / (1.0 - BETA_TWO ** STEP)
    new_master = master - LEARN_RATE * (corrected_one / (jnp.sqrt(corrected_two) + ADAM_EPS) + DECAY_RATE * master)
    return (outputs.reshape(TOKENS, D), grad_inputs.reshape(TOKENS, D), new_master, new_one, new_two)
```

```python
import functools
import math

import jax
import jax.numpy as jnp
import numpy as np
from jax import lax
from jax.experimental import pallas as pl
from jax.experimental.pallas import tpu as pltpu
from jax.sharding import PartitionSpec as P

D = 896
HEADS = 14
KV_HEADS = 2
HEAD = 64
FF = 4864
TREE_LEN = 2048
STEP = 10
RMS_EPS = 1e-06
ROPE_BASE = 1000000.0
BETA_ONE = 0.9
BETA_TWO = 0.95
ADAM_EPS = 1e-08
LEARN_RATE = 0.01
DECAY_RATE = 0.1
NEG_FILL = -1e30
F32 = jnp.float32
BF16 = jnp.bfloat16


ATT=14345; WG0=14345; WD0=82441; G0=116489; END=116503
NFB=38
def up(v,m): return -(-v//m)*m
CH=32
class Plan: pass
def make(dp,ctx,n):
    p=Plan(); O=dp*ctx; p.dp,p.ctx,p.n=dp,ctx,n
    NB=-(-NFB//dp); p.NB=NB
    p.TG=2*D*NB; p.TR=p.TG+NB*896
    r=np.arange(O*n); own=r//n
    so=WD0//n; wd_sp_end=(so+1)*n if WD0%n else WD0
    special=(r<ATT)|((r>=WD0)&(r<wd_sp_end))|((r>=G0)&(r<END))
    pad=r>=END
    gu=(r>=WG0)&(r<WD0); b=np.where(gu,(r-WG0)%NFB,(r-WD0)//896)
    dd=b%dp; slot=b//dp
    t=np.where(gu,((r-WG0)//NFB)*NB+slot,p.TG+slot*896+(r-WD0)%896)
    mlp=~special&~pad
    scount=np.bincount(own[special],minlength=O).reshape(dp,ctx)
    p.ns=[up(-(-int(m)//dp),16) for m in scount.max(1)]
    p.nsm=max(p.ns)
    p.lo=np.concatenate([[0],np.cumsum(p.ns)])[:-1]; p.NL=int(sum(p.ns))
    a=np.zeros((O,dp),np.int64); ln=np.zeros((O,dp),np.int64)
    for o in range(O):
        for d in range(dp):
            m=mlp&(own==o)&(dd==d)
            mm=np.nonzero(m[o*n:(o+1)*n])[0]
            if len(mm):
                tt=t[o*n+mm]; a[o,d]=tt.min()//16*16; ln[o,d]=up(tt.max()+1-a[o,d],CH)
    hs=scount.reshape(-1)>0
    U=0
    for o in range(O):
        U=max(U,int(ln[o].max())+(p.ns[o//ctx] if hs[o] else 0))
    p.U=U=up(U,32)
    fwd=np.full((O,dp*U),n,np.int32); back=np.full((O,n),0,np.int32)
    NBK=dp*U
    p.zero_back=dp*U+dp*p.nsm
    back[:]=p.zero_back
    for o in range(O):
        do=o//ctx; base=o*n
        ro=np.arange(base,base+n)
        m=mlp[ro]
        q=dd[ro]^do
        pos=t[ro]-a[o,dd[ro]%dp]
        k=np.nonzero(m)[0]
        fwd[o,q[k]*U+pos[k]]=k
        back[o,k]=q[k]*U+pos[k]
        k=np.nonzero(special[ro])[0]
        if len(k):
            s=np.arange(len(k)); ns=p.ns[do]
            dprime=s//ns; qq=dprime^do
            fwd[o,qq*U+U-ns+s%ns]=k
            back[o,k]=dp*U+qq*p.nsm+s%ns
    p.fwd,p.back=fwd,back
    aT=np.zeros((dp,ctx,dp),np.int32); nT=np.zeros((dp,ctx,dp),np.int32)
    for d in range(dp):
        for c in range(ctx):
            for q in range(dp):
                o=(d^q)*ctx+c
                aT[d,c,q]=a[o,d]; nT[d,c,q]=ln[o,d]//CH
    p.aT,p.nT=aT.reshape(dp,-1),nT.reshape(dp,-1)
    p.so=[]; off=0
    for o in range(O):
        if hs[o]:
            p.so.append((o,o//ctx,o%ctx,int(scount.reshape(-1)[o]),off)); off+=p.ns[o//ctx]
    p.RS=off
    seg=[]
    for (o,ds,c,cnt,of) in p.so:
        rows=np.nonzero(special[o*n:(o+1)*n])[0]+o*n
        ns=p.ns[ds]
        s=0
        while s<cnt:
            dprime=s//ns; e=min((dprime+1)*ns,cnt)
            x=s
            while x<e:
                y=x+1
                while y<e and rows[y]==rows[y-1]+1 : y+=1
                f0=int(rows[x])
                seg.append((f0,dprime,of+(x%ns),y-x)); x=y
            s=e
    p.seg=seg
    p.att_seg=[s for s in seg if s[0]<ATT]
    p.gain_seg=[s for s in seg if s[0]>=G0]
    wd=[]
    for (f0,dprime,row0,L) in seg:
        if WD0<=f0<G0:
            x=f0
            while x<f0+L:
                bb=(x-WD0)//896; e=min(f0+L,WD0+(bb+1)*896)
                wd.append((bb%dp,p.TG+(bb//dp)*896+(x-WD0)%896,dprime,row0+x-f0,e-x)); x=e
    p.wd_seg=wd
    return p


VM = pltpu.VMEM


def vspec():
    return pl.BlockSpec(memory_space=pltpu.VMEM)


def sspec():
    return pl.BlockSpec(memory_space=pltpu.SMEM)


def aspec():
    return pl.BlockSpec(memory_space=pl.ANY)


def cost(flops, nbytes):
    return pl.CostEstimate(flops=int(flops), bytes_accessed=int(nbytes), transcendentals=0)


def params():
    return pltpu.CompilerParams(vmem_limit_bytes=60 * 1024 * 1024)


def row_loop(count, idx_ref, src_ref, dst_ref):
    def step(j, carry):
        for u in range(16):
            row = j * 16 + u
            dst_ref[pl.ds(row, 1), :] = src_ref[pl.ds(idx_ref[row], 1), :]
        return carry

    lax.fori_loop(0, count // 16, step, 0)


def spread_rows(table, shard):
    n, total = shard.shape[0], table.shape[0]

    def kernel(idx_ref, x_ref, o_ref, xs, os):
        low = n // 8 * 8
        xs[low : low + 16, :] = jnp.zeros((16, 128), F32)
        xs[0:n, :] = x_ref[...]
        row_loop(total, idx_ref, xs, os)
        o_ref[...] = os[...].astype(BF16)

    return pl.pallas_call(
        kernel,
        name="spread_rows",
        out_shape=jax.ShapeDtypeStruct((total, 128), BF16),
        in_specs=[sspec(), vspec()],
        out_specs=vspec(),
        scratch_shapes=[VM((n // 8 * 8 + 16, 128), F32), VM((total, 128), F32)],
        compiler_params=params(),
        cost_estimate=cost(0, total * 4096),
    )(table, shard)


def collect_rows(table, parts, n):
    total = sum(p.shape[0] for p in parts)
    padded = table.shape[0]

    def kernel(idx_ref, *refs):
        ins, o_ref, xs, os = refs[: len(parts)], refs[-3], refs[-2], refs[-1]
        base = 0
        for ref in ins:
            size = ref.shape[0]
            xs[base : base + size, :] = ref[...].astype(F32)
            base += size
        xs[total : total + 8, :] = jnp.zeros((8, 128), F32)
        row_loop(padded, idx_ref, xs, os)
        o_ref[...] = os[0:n, :]

    return pl.pallas_call(
        kernel,
        name="collect_rows",
        out_shape=jax.ShapeDtypeStruct((n, 128), F32),
        in_specs=[sspec()] + [vspec()] * len(parts),
        out_specs=vspec(),
        scratch_shapes=[VM((total + 8, 128), F32), VM((padded, 128), F32)],
        compiler_params=params(),
        cost_estimate=cost(0, padded * 4096),
    )(table, *parts)


def load_attention_weights(p, scal, rel):
    def kernel(s_ref, rel_ref, wqkv, wo, vec, flat):
        d = s_ref[0]
        for f0, dprime, row0, length in p.att_seg:
            flat[f0 : f0 + length, :] = rel_ref[d ^ dprime, row0 : row0 + length, :].astype(F32)
        for q in range(7):
            wqkv[:, 128 * q : 128 * q + 128] = flat[pl.ds(q, D, stride=7), :].astype(BF16)
            wo[:, 128 * q : 128 * q + 128] = flat[pl.ds(8073 + q, D, stride=7), :].astype(BF16)
        wqkv[:, 896:1024] = flat[6279 : 6279 + D, :].astype(BF16)
        wqkv[:, 1024:1152] = flat[7176 : 7176 + D, :].astype(BF16)
        vec[0:7, :] = flat[6272:6279, :]
        vec[7:8, :] = flat[7175:7176, :]
        vec[8:9, :] = flat[8072:8073, :]
        for f0, dprime, row0, length in p.gain_seg:
            g = rel_ref[d ^ dprime, row0 : row0 + up(length, 16), :].astype(F32)
            vec[9 + f0 - G0 : 9 + f0 - G0 + length, :] = g[0:length]

    return pl.pallas_call(
        kernel,
        name="load_attention_weights",
        out_shape=(
            jax.ShapeDtypeStruct((D, 1152), BF16),
            jax.ShapeDtypeStruct((D, D), BF16),
            jax.ShapeDtypeStruct((24, 128), F32),
        ),
        in_specs=[sspec(), vspec()],
        out_specs=(vspec(),) * 3,
        scratch_shapes=[VM((ATT + 7, 128), F32)],
        compiler_params=params(),
        cost_estimate=cost(0, 12e6),
    )(scal, rel)


def store_attention_grads(p, dwqkv, dwo, vec, wdsp):
    def kernel(g_ref, o_ref, v_ref, w_ref, out, flat):
        for q in range(7):
            flat[pl.ds(q, D, stride=7), :] = g_ref[:, 128 * q : 128 * q + 128]
            flat[pl.ds(8073 + q, D, stride=7), :] = o_ref[:, 128 * q : 128 * q + 128]
        flat[6279 : 6279 + D, :] = g_ref[:, 896:1024]
        flat[7176 : 7176 + D, :] = g_ref[:, 1024:1152]
        flat[6272:6279, :] = v_ref[0:7, :]
        flat[7175:7176, :] = v_ref[7:8, :]
        flat[8072:8073, :] = v_ref[8:9, :]
        flat[ATT : ATT + 7, :] = jnp.zeros((7, 128), F32)
        out[...] = jnp.zeros(out.shape, BF16)
        for f0, dprime, row0, length in p.att_seg:
            out[dprime, row0 : row0 + length, :] = flat[f0 : f0 + length, :].astype(BF16)
        for f0, dprime, row0, length in p.gain_seg:
            out[dprime, row0 : row0 + length, :] = v_ref[
                9 + f0 - G0 : 9 + f0 - G0 + length, :
            ].astype(BF16)
        pos = 0
        for _, _, dprime, row0, length in p.wd_seg:
            size = up(length, 16)
            out[dprime, row0 : row0 + size, :] = w_ref[pos : pos + size, :]
            pos += size

    return pl.pallas_call(
        kernel,
        name="store_attention_grads",
        out_shape=jax.ShapeDtypeStruct((p.dp, p.RS, 128), BF16),
        in_specs=[vspec()] * 4,
        out_specs=vspec(),
        scratch_shapes=[VM((ATT + 7, 128), F32)],
        compiler_params=params(),
        cost_estimate=cost(0, 20e6),
    )(dwqkv, dwo, vec, wdsp)


def load_mlp_weights(p, scal, a_tab, n_tab, pieces, rel):
    width = p.NB * 128
    count = p.ctx * p.dp

    def kernel(s_ref, a_ref, n_ref, piece_ref, rel_ref, wgu, wd, tall, stage):
        d = s_ref[0]

        def clear(j, carry):
            tall[pl.ds(pl.multiple_of(j * 128, 128), 128), :] = jnp.zeros((128, 128), BF16)
            return carry

        lax.fori_loop(0, p.TR // 128, clear, 0)

        def one_piece(j, carry):
            base = a_ref[j]

            def one_chunk(k, inner):
                at = pl.multiple_of(base + k * CH, 16)
                frm = pl.multiple_of(k * CH, CH)
                tall[pl.ds(at, CH), :] = tall[pl.ds(at, CH), :] + piece_ref[j, pl.ds(frm, CH), :]
                return inner

            return lax.fori_loop(0, n_ref[j], one_chunk, carry)

        lax.fori_loop(0, count, one_piece, 0)
        for dest, t0, dprime, row0, length in p.wd_seg:

            @pl.when(d == dest)
            def _():
                size = up(length, 16)
                tall[t0 : t0 + size, :] = (
                    tall[t0 : t0 + size, :] + rel_ref[d ^ dprime, row0 : row0 + size, :]
                )

        per = 128 * p.NB

        def gu(j, carry):
            at = pl.multiple_of(j * per, 128)
            stage[0:per, :] = tall[pl.ds(at, per), :].astype(F32)
            row = pl.multiple_of(j * 128, 128)
            for s in range(p.NB):
                wgu[pl.ds(row, 128), 128 * s : 128 * s + 128] = stage[
                    pl.ds(s, 128, stride=p.NB), :
                ].astype(BF16)
            return carry

        lax.fori_loop(0, 2 * D // 128, gu, 0)

        def down(j, carry):
            at = pl.multiple_of(p.TG + j * 896, 128)
            stage[0:896, :] = tall[pl.ds(at, 896), :].astype(F32)
            row = pl.multiple_of(j * 128, 128)
            for s in range(7):
                wd[pl.ds(row, 128), 128 * s : 128 * s + 128] = stage[
                    pl.ds(s, 128, stride=7), :
                ].astype(BF16)
            return carry

        lax.fori_loop(0, p.NB, down, 0)

    return pl.pallas_call(
        kernel,
        name="load_mlp_weights",
        out_shape=(
            jax.ShapeDtypeStruct((2 * D, width), BF16),
            jax.ShapeDtypeStruct((width, D), BF16),
        ),
        in_specs=[sspec()] * 3 + [vspec()] * 2,
        out_specs=(vspec(),) * 2,
        scratch_shapes=[
            VM((p.TR + p.U, 128), BF16),
            VM((max(128 * p.NB, 896), 128), F32),
        ],
        compiler_params=params(),
        cost_estimate=cost(0, 40e6),
    )(scal, a_tab, n_tab, pieces, rel)


def store_mlp_grads(p, scal, a_tab, dwgu, dwd):
    count = p.ctx * p.dp
    per = 128 * p.NB
    sizes = [up(s[4], 16) for s in p.wd_seg]
    total = max(sum(sizes), 16)
    steps_g = 2 * D // 128
    steps = steps_g + p.NB

    def kernel(s_ref, a_ref, g_ref, w_ref, pieces, wdsp, tall, stage, sem):
        d = s_ref[0]
        step = pl.program_id(0)

        @pl.when(step == 0)
        def _():
            tall[p.TR : p.TR + p.U, :] = jnp.zeros((p.U, 128), BF16)

        @pl.when(step < steps_g)
        def _():
            for s in range(p.NB):
                stage[pl.ds(s, 128, stride=p.NB), :] = g_ref[:, 128 * s : 128 * s + 128]
            at = pl.multiple_of(step * per, 128)
            tall[pl.ds(at, per), :] = stage[0:per, :].astype(BF16)

        @pl.when(step >= steps_g)
        def _():
            for s in range(7):
                stage[pl.ds(s, 128, stride=7), :] = w_ref[:, 128 * s : 128 * s + 128]
            at = pl.multiple_of(p.TG + (step - steps_g) * 896, 128)
            tall[pl.ds(at, 896), :] = stage[0:896, :].astype(BF16)

        @pl.when(step == steps - 1)
        def _():
            def copy_of(j):
                at = pl.multiple_of(a_ref[j], 16)
                return pltpu.make_async_copy(tall.at[pl.ds(at, p.U), :], pieces.at[j], sem.at[j])

            def start(j, carry):
                copy_of(j).start()
                return carry

            def wait(j, carry):
                copy_of(j).wait()
                return carry

            lax.fori_loop(0, count, start, 0)
            wdsp[...] = jnp.zeros(wdsp.shape, BF16)
            pos = 0
            for (dest, t0, _, _, _), size in zip(p.wd_seg, sizes):

                @pl.when(d == dest)
                def _():
                    wdsp[pos : pos + size, :] = tall[t0 : t0 + size, :]

                pos += size
            lax.fori_loop(0, count, wait, 0)

    return pl.pallas_call(
        kernel,
        name="store_mlp_grads",
        grid=(steps,),
        out_shape=(
            jax.ShapeDtypeStruct((count, p.U, 128), BF16),
            jax.ShapeDtypeStruct((total, 128), BF16),
        ),
        in_specs=[
            sspec(),
            sspec(),
            pl.BlockSpec((128, per), lambda i: (jnp.minimum(i, steps_g - 1), 0)),
            pl.BlockSpec((128, D), lambda i: (jnp.maximum(i - steps_g, 0), 0)),
        ],
        out_specs=(aspec(), pl.BlockSpec((total, 128), lambda i: (0, 0))),
        scratch_shapes=[
            VM((p.TR + p.U, 128), BF16),
            VM((max(per, 896), 128), F32),
            pltpu.SemaphoreType.DMA((count,)),
        ],
        compiler_params=params(),
        cost_estimate=cost(0, 40e6),
    )(scal, a_tab, dwgu, dwd)


def lane_low(shape):
    return lax.broadcasted_iota(jnp.int32, shape, len(shape) - 1) < HEAD


def half_variants(x, out):
    xf = x.astype(F32)
    rolled = pltpu.roll(xf, HEAD, 1)
    low = lane_low(xf.shape)
    out[0] = jnp.where(low, xf, 0.0).astype(BF16)
    out[1] = jnp.where(low, 0.0, rolled).astype(BF16)
    out[2] = jnp.where(low, rolled, 0.0).astype(BF16)
    out[3] = jnp.where(low, 0.0, xf).astype(BF16)


def half_variants_t(xt, out):
    xf = xt.astype(F32)
    swapped = jnp.concatenate([xf[HEAD:], xf[:HEAD]], axis=0)
    low = lax.broadcasted_iota(jnp.int32, xf.shape, 0) < HEAD
    out[0] = jnp.where(low, xf, 0.0).astype(BF16)
    out[1] = jnp.where(low, 0.0, swapped).astype(BF16)
    out[2] = jnp.where(low, swapped, 0.0).astype(BF16)
    out[3] = jnp.where(low, 0.0, xf).astype(BF16)


def dot(a, b):
    return jnp.dot(a, b, preferred_element_type=F32)


def attention_forward(q_t, keys, values_t, bias):
    toks, length = q_t.shape[1], keys.shape[0]
    groups = HEADS // KV_HEADS

    def kernel(q_ref, k_ref, v_ref, b_ref, o_ref, l_ref, kvar, vvar):
        blk = pl.program_id(0)

        @pl.when(blk == 0)
        def _():
            half_variants(k_ref[...], kvar)
            half_variants_t(v_ref[...], vvar)

        acc = None
        for half in range(2):
            var = 2 * ((2 * blk + half) // groups) + half
            s = dot(kvar[var], q_ref[...]) + b_ref[...]
            peak = jnp.max(s, axis=0, keepdims=True)
            e = jnp.exp(s - peak)
            total = jnp.sum(e, axis=0, keepdims=True)
            probs = (e * (1.0 / total)).astype(BF16)
            part = dot(vvar[var], probs)
            acc = part if acc is None else acc + part
            l_ref[0, half : half + 1, :] = peak + jnp.log(total)
        o_ref[...] = acc.T

    return pl.pallas_call(
        kernel,
        name="attention_forward",
        grid=(7,),
        out_shape=(
            jax.ShapeDtypeStruct((toks, D), F32),
            jax.ShapeDtypeStruct((7, 8, toks), F32),
        ),
        in_specs=[pl.BlockSpec((128, toks), lambda i: (i, 0)), vspec(), vspec(), vspec()],
        out_specs=(
            pl.BlockSpec((toks, 128), lambda i: (0, i)),
            pl.BlockSpec((1, 8, toks), lambda i: (i, 0, 0)),
        ),
        scratch_shapes=[VM((4, length, 128), BF16), VM((4, 128, length), BF16)],
        compiler_params=params(),
        cost_estimate=cost(8 * 14 * 256 * 2048 * 128, 4e6),
    )(q_t, keys, values_t, bias)


def attention_backward(q_t, q, do_t, do, keys, keys_t, values, bias, lse, delta):
    toks, length = q_t.shape[1], keys.shape[0]
    groups = HEADS // KV_HEADS

    def kernel(
        qt_ref, q_ref, dot_ref, do_ref, k_ref, kt_ref, v_ref, b_ref, l_ref, d_ref,
        dq_ref, dk_ref, dv_ref, kvar, ktvar, vvar, dk_acc, dv_acc,
    ):
        blk = pl.program_id(0)

        @pl.when(blk == 0)
        def _():
            half_variants(k_ref[...], kvar)
            half_variants(v_ref[...], vvar)
            half_variants_t(kt_ref[...], ktvar)
            dk_acc[...] = jnp.zeros(dk_acc.shape, F32)
            dv_acc[...] = jnp.zeros(dv_acc.shape, F32)

        low = lane_low((toks, 128))
        acc = None
        for half in range(2):
            group = (2 * blk + half) // groups
            var = 2 * group + half
            keep = low if half == 0 else jnp.logical_not(low)
            q_half = jnp.where(keep, q_ref[...].astype(F32), 0.0).astype(BF16)
            do_half = jnp.where(keep, do_ref[...].astype(F32), 0.0).astype(BF16)
            s = dot(kvar[var], qt_ref[...]) + b_ref[...]
            prob = jnp.exp(s - l_ref[0, half : half + 1, :])
            dv_acc[group] += dot(prob.astype(BF16), do_half)
            dp = dot(vvar[var], dot_ref[...])
            ds = (prob * (dp - d_ref[0, half : half + 1, :])).astype(BF16)
            dk_acc[group] += dot(ds, q_half)
            part = dot(ktvar[var], ds)
            acc = part if acc is None else acc + part
        dq_ref[...] = acc.T

        @pl.when(blk == 6)
        def _():
            lowk = lane_low((length, 128))
            for a_ref, o_ref in ((dk_acc, dk_ref), (dv_acc, dv_ref)):
                one, two = a_ref[0], a_ref[1]
                one = one + pltpu.roll(one, HEAD, 1)
                two = two + pltpu.roll(two, HEAD, 1)
                o_ref[...] = jnp.where(lowk, one, two)

    return pl.pallas_call(
        kernel,
        name="attention_backward",
        grid=(7,),
        out_shape=(
            jax.ShapeDtypeStruct((toks, D), F32),
            jax.ShapeDtypeStruct((length, 128), F32),
            jax.ShapeDtypeStruct((length, 128), F32),
        ),
        in_specs=[
            pl.BlockSpec((128, toks), lambda i: (i, 0)),
            pl.BlockSpec((toks, 128), lambda i: (0, i)),
            pl.BlockSpec((128, toks), lambda i: (i, 0)),
            pl.BlockSpec((toks, 128), lambda i: (0, i)),
            vspec(), vspec(), vspec(), vspec(),
            pl.BlockSpec((1, 8, toks), lambda i: (i, 0, 0)),
            pl.BlockSpec((1, 8, toks), lambda i: (i, 0, 0)),
        ],
        out_specs=(
            pl.BlockSpec((toks, 128), lambda i: (0, i)),
            pl.BlockSpec((length, 128), lambda i: (0, 0)),
            pl.BlockSpec((length, 128), lambda i: (0, 0)),
        ),
        scratch_shapes=[
            VM((4, length, 128), BF16),
            VM((4, 128, length), BF16),
            VM((4, length, 128), BF16),
            VM((2, length, 128), F32),
            VM((2, length, 128), F32),
        ],
        compiler_params=params(),
        cost_estimate=cost(20 * 14 * 256 * 2048 * 128, 8e6),
    )(q_t, q, do_t, do, keys, keys_t, values, bias, lse, delta)


def rms_scale(values):
    return lax.rsqrt(jnp.mean(values * values, axis=-1, keepdims=True) + RMS_EPS)


def rms_back(values, scale_vals, gain, grad_out):
    unit_vals = values * scale_vals
    gain_grad = jnp.sum(grad_out * unit_vals, axis=0)
    grad_unit = grad_out * gain
    inner = jnp.mean(grad_unit * unit_vals, axis=-1, keepdims=True)
    return (scale_vals * (grad_unit - unit_vals * inner), gain_grad)


def rope_tables(positions):
    half_dim = HEAD // 2
    inverse = ROPE_BASE ** (-(jnp.arange(half_dim, dtype=F32) * 2.0 / HEAD))
    angles = positions.astype(F32)[:, None] * inverse[None, :]
    return jnp.cos(angles)[:, None, :], jnp.sin(angles)[:, None, :]


def rotate(values, tables, sign):
    cosine, sine = tables
    sine = sine * sign
    first = values[..., : HEAD // 2]
    second = values[..., HEAD // 2 :]
    return jnp.concatenate(
        [first * cosine - second * sine, second * cosine + first * sine], axis=-1
    )


def ancestor_bits(parents):
    tree_count, seg_count = parents.shape
    current = jnp.broadcast_to(
        jnp.arange(seg_count, dtype=jnp.int32)[None, :], (tree_count, seg_count)
    )
    bits = jnp.zeros((tree_count, seg_count), jnp.int32)
    hot = jnp.arange(seg_count, dtype=jnp.int32)
    for _ in range(seg_count):
        bits = jnp.bitwise_or(bits, jnp.left_shift(jnp.ones_like(current), current))
        pick = current[:, :, None] == hot[None, None, :]
        current = jnp.sum(jnp.where(pick, parents[:, None, :], 0), axis=2)
    return bits


def swap(x, axis, size, mask):
    return lax.ppermute(x, axis, [(i, i ^ mask) for i in range(size)])


def body(p, inputs, cotangent, parents, lengths, positions, master, moment_one, moment_two):
    toks = inputs.shape[0]
    dp, ctx, n, U = p.dp, p.ctx, p.n, p.U
    d, c = lax.axis_index("dp"), lax.axis_index("ctx")
    core = jnp.bitwise_and(c, 1)
    scal = d.reshape(1).astype(jnp.int32)
    owner = d * ctx + c

    def pick(table, i):
        return lax.dynamic_index_in_dim(jnp.asarray(table), i, 0, keepdims=False)

    def dyn(x, i):
        return lax.dynamic_index_in_dim(x, i, 0, keepdims=False)

    a_tab, n_tab = pick(p.aT, d), pick(p.nT, d)
    pieces = spread_rows(pick(p.fwd, owner), master).reshape(dp, U, 128)
    got = [pieces[0]] + [swap(pieces[q], "dp", dp, q) for q in range(1, dp)]
    gathered = jnp.stack(got)
    late = jnp.concatenate(
        [dyn(gathered, d ^ s)[U - p.ns[s] :] for s in range(dp) if p.ns[s]], axis=0
    )
    late_all = lax.all_gather(late, "ctx", axis=0)
    gathered, late_all = lax.optimization_barrier((gathered, late_all))
    mlp_pieces = lax.all_gather(gathered, "ctx", axis=0)
    sp_own = jnp.concatenate(
        [late_all[cc, p.lo[s] : p.lo[s] + p.ns[s]] for (_, s, cc, _, _) in p.so], axis=0
    )
    half_rows = p.RS // 2
    sp_half = lax.dynamic_slice_in_dim(sp_own, core * half_rows, half_rows, 0)
    mine = jnp.stack([swap(sp_half, "dp", dp, q) for q in range(1, dp)])
    theirs = swap(mine, "ctx", ctx, 1)
    first = jnp.where(core == 0, mine, theirs)
    second_half = jnp.where(core == 0, theirs, mine)
    rel = jnp.concatenate([sp_own[None], jnp.concatenate([first, second_half], axis=1)], axis=0)
    w_qkv, w_out, vec = load_attention_weights(p, scal, rel)
    bias_qkv = vec[0:9].reshape(1152)
    norm_one, norm_two = vec[9:16].reshape(D), vec[16:23].reshape(D)

    per_tree = TREE_LEN // toks
    z_count = per_tree // 2
    bits_all = ancestor_bits(parents)
    ends_all = jnp.cumsum(lengths, axis=1)
    tree = c // per_tree
    ends, bits = dyn(ends_all, tree), dyn(bits_all, tree)

    def seg_of(index):
        return jnp.sum((index[:, None] >= ends[None, :]).astype(jnp.int32), axis=1)

    tok_iota = jnp.arange(toks, dtype=jnp.int32)
    q_idx = (c % per_tree) * toks + tok_iota
    k_idx = jnp.concatenate(
        [
            ((c ^ (2 * q) ^ r) % per_tree) * toks + tok_iota
            for r in range(2)
            for q in range(z_count)
        ]
    )
    q_seg, k_seg = seg_of(q_idx), seg_of(k_idx)
    seg_iota = jnp.arange(ends.shape[0], dtype=jnp.int32)
    q_bits = jnp.sum(jnp.where(q_seg[:, None] == seg_iota[None, :], bits[None, :], 0), axis=1)
    allowed = (jnp.right_shift(q_bits[None, :], k_seg[:, None]) & 1 == 1) & (
        k_idx[:, None] <= q_idx[None, :]
    )
    bias = jnp.where(allowed, 0.0, NEG_FILL).astype(F32)
    tables = rope_tables(positions)
    cots = jnp.concatenate(
        [cotangent] + [swap(cotangent, "dp", dp, q) for q in range(1, dp)], axis=0
    )

    x = inputs.astype(F32)
    scale_one = rms_scale(x)
    normed = (x * scale_one * norm_one).astype(BF16)
    qkv = dot(normed, w_qkv) + bias_qkv
    query = rotate(qkv[:, :D].reshape(toks, HEADS, HEAD), tables, 1.0).reshape(toks, D)
    query = query.astype(BF16) * jnp.asarray(HEAD**-0.5, BF16)
    key = rotate(qkv[:, D : D + 128].reshape(toks, KV_HEADS, HEAD), tables, 1.0)
    kv = jnp.concatenate(
        [key.reshape(toks, 128).astype(BF16), qkv[:, D + 128 :].astype(BF16)], axis=1
    )
    kv_own = jnp.stack([kv] + [swap(kv, "ctx", ctx, 2 * q) for q in range(1, z_count)])
    kv_all = jnp.concatenate([kv_own, swap(kv_own, "ctx", ctx, 1)]).reshape(TREE_LEN, 256)
    keys, values = kv_all[:, :128], kv_all[:, 128:]
    q_t = query.T
    attended, lse = attention_forward(q_t, keys, values.T, bias)
    attended_b = attended.astype(BF16)
    middle = x + dot(attended_b, w_out)
    scale_two = rms_scale(middle)
    second = (middle * scale_two * norm_two).astype(BF16)

    w_gu, w_down = load_mlp_weights(
        p, scal, a_tab, n_tab, mlp_pieces.reshape(ctx * dp, U, 128), rel
    )
    w_gate, w_up = w_gu[:D], w_gu[D:]
    seconds = jnp.concatenate(
        [second] + [swap(second, "dp", dp, q) for q in range(1, dp)], axis=0
    )

    def back_to_owner(part):
        blocks = part.reshape(dp, toks, D)
        total = blocks[0]
        for q in range(1, dp):
            total = total + swap(blocks[q].astype(BF16), "dp", dp, q).astype(F32)
        return total

    gate = dot(seconds, w_gate)
    up_act = dot(seconds, w_up)
    gate_sig = jax.nn.sigmoid(gate)
    hidden = (gate * gate_sig * up_act).astype(BF16)
    d_hidden = jnp.einsum("td,fd->tf", cots, w_down, preferred_element_type=F32)
    d_gate = (d_hidden * up_act * gate_sig * (1.0 + gate * (1.0 - gate_sig))).astype(BF16)
    d_up = (d_hidden * gate * gate_sig).astype(BF16)
    d_second_part = jnp.einsum(
        "tf,df->td", d_gate, w_gate, preferred_element_type=F32
    ) + jnp.einsum("tf,df->td", d_up, w_up, preferred_element_type=F32)
    d_second = back_to_owner(d_second_part)
    activations = (middle + back_to_owner(dot(hidden, w_down))).astype(BF16)
    dw_gate = jnp.einsum("td,tf->df", seconds, d_gate, preferred_element_type=F32)
    dw_up = jnp.einsum("td,tf->df", seconds, d_up, preferred_element_type=F32)
    dw_down = jnp.einsum("tf,td->fd", hidden, cots, preferred_element_type=F32)
    grad_pieces, wd_special = store_mlp_grads(
        p, scal, a_tab, jnp.concatenate([dw_gate, dw_up], axis=0), dw_down
    )
    own_pieces = lax.psum_scatter(
        grad_pieces.reshape(ctx, dp, U, 128), "ctx", scatter_dimension=0, tiled=False
    )

    middle_norm_grad, gain_two_grad = rms_back(middle, scale_two, norm_two, d_second)
    middle_grad = cotangent.astype(F32) + middle_norm_grad
    branch = middle_grad.astype(BF16)
    dw_out = jnp.einsum("th,td->hd", attended_b, branch, preferred_element_type=F32)
    d_out = jnp.einsum("td,hd->th", branch, w_out, preferred_element_type=F32).astype(BF16)
    delta = jnp.sum((d_out.astype(F32) * attended).reshape(toks, HEADS, HEAD), axis=-1)
    delta = jnp.pad(delta.T.reshape(7, 2, toks), ((0, 0), (0, 6), (0, 0)))
    d_query, d_key, d_value = attention_backward(
        q_t, query, d_out.T, d_out, keys, keys.T, values, bias, lse, delta
    )
    d_kv = jnp.concatenate([d_key, d_value], axis=1).reshape(2, z_count, toks, 256)
    d_kv = d_kv[0] + swap(d_kv[1].astype(BF16), "ctx", ctx, 1).astype(F32)
    kv_grad = d_kv[0]
    for q in range(1, z_count):
        kv_grad = kv_grad + swap(d_kv[q].astype(BF16), "ctx", ctx, 2 * q).astype(F32)
    dq_pre = rotate((d_query * HEAD**-0.5).reshape(toks, HEADS, HEAD), tables, -1.0)
    dk_pre = rotate(
        kv_grad[:, :128].astype(BF16).astype(F32).reshape(toks, KV_HEADS, HEAD), tables, -1.0
    )
    d_qkv = jnp.concatenate(
        [dq_pre.reshape(toks, D), dk_pre.reshape(toks, 128), kv_grad[:, 128:]], axis=1
    ).astype(BF16)
    dw_qkv = jnp.einsum("td,th->dh", normed, d_qkv, preferred_element_type=F32)
    db_qkv = jnp.sum(d_qkv.astype(F32), axis=0)
    d_normed = jnp.einsum("th,dh->td", d_qkv, w_qkv, preferred_element_type=F32)
    input_norm_grad, gain_one_grad = rms_back(x, scale_one, norm_one, d_normed)
    input_grad = middle_grad + input_norm_grad

    vec_grad = jnp.concatenate(
        [db_qkv, gain_one_grad, gain_two_grad, jnp.zeros((128,), F32)]
    ).reshape(24, 128)
    sp_grad = store_attention_grads(p, dw_qkv, dw_out, vec_grad, wd_special)
    keep = lax.dynamic_slice_in_dim(sp_grad, core * half_rows, half_rows, 1)
    give = lax.dynamic_slice_in_dim(sp_grad, (1 - core) * half_rows, half_rows, 1)
    pair = (keep.astype(F32) + swap(give, "ctx", ctx, 1).astype(F32)).astype(BF16)
    chunk = dyn(pair, d).astype(F32)
    for q in range(1, dp):
        chunk = chunk + swap(dyn(pair, d ^ q), "dp", dp, q).astype(F32)
    chunk = lax.dynamic_update_slice_in_dim(
        jnp.zeros((p.RS, 128), BF16), chunk.astype(BF16), core * half_rows, 0
    )
    offset_of = {(s, cc): off for (_, s, cc, _, off) in p.so}
    rows = []
    for cc in range(ctx):
        for s in range(dp):
            if p.ns[s]:
                if (s, cc) in offset_of:
                    off = offset_of[(s, cc)]
                    rows.append(chunk[off : off + p.ns[s]])
                else:
                    rows.append(jnp.zeros((p.ns[s], 128), BF16))
    late_grad = lax.psum_scatter(
        jnp.concatenate(rows, axis=0).reshape(ctx, p.NL, 128),
        "ctx",
        scatter_dimension=0,
        tiled=False,
    )
    late_grad = jnp.pad(late_grad, ((0, p.nsm), (0, 0)))

    def late_for(q):
        return lax.dynamic_slice_in_dim(late_grad, pick(p.lo.astype(np.int32), d ^ q), p.nsm, 0)

    parts = [dyn(own_pieces, jnp.int32(0))]
    parts += [swap(own_pieces[q], "dp", dp, q) for q in range(1, dp)]
    parts += [late_for(0)] + [swap(late_for(q), "dp", dp, q) for q in range(1, dp)]
    own_grad = collect_rows(pick(p.back_padded, owner), parts, n)
    own_grad = own_grad * (toks * dp * ctx) ** (-0.5)
    new_one = BETA_ONE * moment_one + (1.0 - BETA_ONE) * own_grad
    new_two = BETA_TWO * moment_two + (1.0 - BETA_TWO) * own_grad * own_grad
    corrected_one = new_one / (1.0 - BETA_ONE**STEP)
    corrected_two = new_two / (1.0 - BETA_TWO**STEP)
    new_master = master - LEARN_RATE * (
        corrected_one / (jnp.sqrt(corrected_two) + ADAM_EPS) + DECAY_RATE * master
    )
    return (activations, input_grad, new_master, new_one, new_two)


def solution(mesh):
    dp, ctx = mesh.shape["dp"], mesh.shape["ctx"]

    def run(inputs, cotangent, parents, lengths, positions, master, moment_one, moment_two):
        n = master.shape[0] // (dp * ctx)
        p = make(dp, ctx, n)
        extra = up(n, 16) - n
        p.back_padded = np.pad(p.back, ((0, 0), (0, extra)), constant_values=p.zero_back)
        row = P(("dp", "ctx"), None)
        step = jax.shard_map(
            functools.partial(body, p),
            mesh=mesh,
            in_specs=(row, row, P("dp", None), P("dp", None), P(("dp", "ctx")), row, row, row),
            out_specs=(row,) * 5,
            check_vma=False,
        )
        return step(
            inputs, cotangent, parents, lengths, positions, master, moment_one, moment_two
        )

    return run
```

```python
import functools
import math

import jax
import jax.numpy as jnp
import numpy as np
from jax import lax
from jax.experimental import pallas as pl
from jax.experimental.pallas import tpu as pltpu
from jax.sharding import PartitionSpec as P

D = 896
HEADS = 14
KV_HEADS = 2
HEAD = 64
FF = 4864
TREE_LEN = 2048
STEP = 10
RMS_EPS = 1e-06
ROPE_BASE = 1000000.0
BETA_ONE = 0.9
BETA_TWO = 0.95
ADAM_EPS = 1e-08
LEARN_RATE = 0.01
DECAY_RATE = 0.1
NEG_FILL = -1e30
F32 = jnp.float32
BF16 = jnp.bfloat16


ATT=14345; WG0=14345; WD0=82441; G0=116489; END=116503
NFB=38
def up(v,m): return -(-v//m)*m
CH=32
class Plan: pass
def make(dp,ctx,n):
    p=Plan(); O=dp*ctx; p.dp,p.ctx,p.n=dp,ctx,n
    NB=-(-NFB//dp); p.NB=NB
    p.TG=2*D*NB; p.TR=p.TG+NB*896
    r=np.arange(O*n); own=r//n
    so=WD0//n; wd_sp_end=(so+1)*n if WD0%n else WD0
    special=(r<ATT)|((r>=WD0)&(r<wd_sp_end))|((r>=G0)&(r<END))
    pad=r>=END
    gu=(r>=WG0)&(r<WD0); b=np.where(gu,(r-WG0)%NFB,(r-WD0)//896)
    dd=b%dp; slot=b//dp
    t=np.where(gu,((r-WG0)//NFB)*NB+slot,p.TG+slot*896+(r-WD0)%896)
    mlp=~special&~pad
    scount=np.bincount(own[special],minlength=O).reshape(dp,ctx)
    p.ns=[up(-(-int(m)//dp),16) for m in scount.max(1)]
    p.nsm=max(p.ns)
    p.lo=np.concatenate([[0],np.cumsum(p.ns)])[:-1]; p.NL=int(sum(p.ns))
    a=np.zeros((O,dp),np.int64); ln=np.zeros((O,dp),np.int64)
    for o in range(O):
        for d in range(dp):
            m=mlp&(own==o)&(dd==d)
            mm=np.nonzero(m[o*n:(o+1)*n])[0]
            if len(mm):
                tt=t[o*n+mm]; a[o,d]=tt.min()//16*16; ln[o,d]=up(tt.max()+1-a[o,d],CH)
    hs=scount.reshape(-1)>0
    U=0
    for o in range(O):
        U=max(U,int(ln[o].max())+(p.ns[o//ctx] if hs[o] else 0))
    p.U=U=up(U,32)
    fwd=np.full((O,dp*U),n,np.int32); back=np.full((O,n),0,np.int32)
    NBK=dp*U
    p.zero_back=dp*U+dp*p.nsm
    back[:]=p.zero_back
    for o in range(O):
        do=o//ctx; base=o*n
        ro=np.arange(base,base+n)
        m=mlp[ro]
        q=dd[ro]^do
        pos=t[ro]-a[o,dd[ro]%dp]
        k=np.nonzero(m)[0]
        fwd[o,q[k]*U+pos[k]]=k
        back[o,k]=q[k]*U+pos[k]
        k=np.nonzero(special[ro])[0]
        if len(k):
            s=np.arange(len(k)); ns=p.ns[do]
            dprime=s//ns; qq=dprime^do
            fwd[o,qq*U+U-ns+s%ns]=k
            back[o,k]=dp*U+qq*p.nsm+s%ns
    p.fwd,p.back=fwd,back
    aT=np.zeros((dp,ctx,dp),np.int32); nT=np.zeros((dp,ctx,dp),np.int32)
    for d in range(dp):
        for c in range(ctx):
            for q in range(dp):
                o=(d^q)*ctx+c
                aT[d,c,q]=a[o,d]; nT[d,c,q]=ln[o,d]//CH
    p.aT,p.nT=aT.reshape(dp,-1),nT.reshape(dp,-1)
    p.so=[]; off=0
    for o in range(O):
        if hs[o]:
            p.so.append((o,o//ctx,o%ctx,int(scount.reshape(-1)[o]),off)); off+=p.ns[o//ctx]
    p.RS=off
    seg=[]
    for (o,ds,c,cnt,of) in p.so:
        rows=np.nonzero(special[o*n:(o+1)*n])[0]+o*n
        ns=p.ns[ds]
        s=0
        while s<cnt:
            dprime=s//ns; e=min((dprime+1)*ns,cnt)
            x=s
            while x<e:
                y=x+1
                while y<e and rows[y]==rows[y-1]+1 : y+=1
                f0=int(rows[x])
                seg.append((f0,dprime,of+(x%ns),y-x)); x=y
            s=e
    p.seg=seg
    p.att_seg=[s for s in seg if s[0]<ATT]
    p.gain_seg=[s for s in seg if s[0]>=G0]
    wd=[]
    for (f0,dprime,row0,L) in seg:
        if WD0<=f0<G0:
            x=f0
            while x<f0+L:
                bb=(x-WD0)//896; e=min(f0+L,WD0+(bb+1)*896)
                wd.append((bb%dp,p.TG+(bb//dp)*896+(x-WD0)%896,dprime,row0+x-f0,e-x)); x=e
    p.wd_seg=wd
    return p


VM = pltpu.VMEM


def vspec():
    return pl.BlockSpec(memory_space=pltpu.VMEM)


def sspec():
    return pl.BlockSpec(memory_space=pltpu.SMEM)


def aspec():
    return pl.BlockSpec(memory_space=pl.ANY)


def cost(flops, nbytes):
    return pl.CostEstimate(flops=int(flops), bytes_accessed=int(nbytes), transcendentals=0)


def params():
    return pltpu.CompilerParams(vmem_limit_bytes=60 * 1024 * 1024)


def row_loop(count, idx_ref, src_ref, dst_ref):
    def step(j, carry):
        for u in range(16):
            row = j * 16 + u
            dst_ref[pl.ds(row, 1), :] = src_ref[pl.ds(idx_ref[row], 1), :]
        return carry

    lax.fori_loop(0, count // 16, step, 0)


def spread_rows(table, shard):
    n, total = shard.shape[0], table.shape[0]

    def kernel(idx_ref, x_ref, o_ref, xs, os):
        low = n // 8 * 8
        xs[low : low + 16, :] = jnp.zeros((16, 128), F32)
        xs[0:n, :] = x_ref[...]
        row_loop(total, idx_ref, xs, os)
        o_ref[...] = os[...].astype(BF16)

    return pl.pallas_call(
        kernel,
        name="spread_rows",
        out_shape=jax.ShapeDtypeStruct((total, 128), BF16),
        in_specs=[sspec(), vspec()],
        out_specs=vspec(),
        scratch_shapes=[VM((n // 8 * 8 + 16, 128), F32), VM((total, 128), F32)],
        compiler_params=params(),
        cost_estimate=cost(0, total * 4096),
    )(table, shard)


def collect_rows(table, parts, n):
    total = sum(p.shape[0] for p in parts)
    padded = table.shape[0]

    def kernel(idx_ref, *refs):
        ins, o_ref, xs, os = refs[: len(parts)], refs[-3], refs[-2], refs[-1]
        base = 0
        for ref in ins:
            size = ref.shape[0]
            xs[base : base + size, :] = ref[...].astype(F32)
            base += size
        xs[total : total + 8, :] = jnp.zeros((8, 128), F32)
        row_loop(padded, idx_ref, xs, os)
        o_ref[...] = os[0:n, :]

    return pl.pallas_call(
        kernel,
        name="collect_rows",
        out_shape=jax.ShapeDtypeStruct((n, 128), F32),
        in_specs=[sspec()] + [vspec()] * len(parts),
        out_specs=vspec(),
        scratch_shapes=[VM((total + 8, 128), F32), VM((padded, 128), F32)],
        compiler_params=params(),
        cost_estimate=cost(0, padded * 4096),
    )(table, *parts)


def load_attention_weights(p, scal, rel):
    def kernel(s_ref, rel_ref, wqkv, wo, vec, flat):
        d = s_ref[0]
        for f0, dprime, row0, length in p.att_seg:
            flat[f0 : f0 + length, :] = rel_ref[d ^ dprime, row0 : row0 + length, :].astype(F32)
        for q in range(7):
            wqkv[:, 128 * q : 128 * q + 128] = flat[pl.ds(q, D, stride=7), :].astype(BF16)
            wo[:, 128 * q : 128 * q + 128] = flat[pl.ds(8073 + q, D, stride=7), :].astype(BF16)
        wqkv[:, 896:1024] = flat[6279 : 6279 + D, :].astype(BF16)
        wqkv[:, 1024:1152] = flat[7176 : 7176 + D, :].astype(BF16)
        vec[0:7, :] = flat[6272:6279, :]
        vec[7:8, :] = flat[7175:7176, :]
        vec[8:9, :] = flat[8072:8073, :]
        for f0, dprime, row0, length in p.gain_seg:
            g = rel_ref[d ^ dprime, row0 : row0 + up(length, 16), :].astype(F32)
            vec[9 + f0 - G0 : 9 + f0 - G0 + length, :] = g[0:length]

    return pl.pallas_call(
        kernel,
        name="load_attention_weights",
        out_shape=(
            jax.ShapeDtypeStruct((D, 1152), BF16),
            jax.ShapeDtypeStruct((D, D), BF16),
            jax.ShapeDtypeStruct((24, 128), F32),
        ),
        in_specs=[sspec(), vspec()],
        out_specs=(vspec(),) * 3,
        scratch_shapes=[VM((ATT + 7, 128), F32)],
        compiler_params=params(),
        cost_estimate=cost(0, 12e6),
    )(scal, rel)


def store_attention_grads(p, dwqkv, dwo, vec, wdsp):
    def kernel(g_ref, o_ref, v_ref, w_ref, out, flat):
        for q in range(7):
            flat[pl.ds(q, D, stride=7), :] = g_ref[:, 128 * q : 128 * q + 128]
            flat[pl.ds(8073 + q, D, stride=7), :] = o_ref[:, 128 * q : 128 * q + 128]
        flat[6279 : 6279 + D, :] = g_ref[:, 896:1024]
        flat[7176 : 7176 + D, :] = g_ref[:, 1024:1152]
        flat[6272:6279, :] = v_ref[0:7, :]
        flat[7175:7176, :] = v_ref[7:8, :]
        flat[8072:8073, :] = v_ref[8:9, :]
        flat[ATT : ATT + 7, :] = jnp.zeros((7, 128), F32)
        out[...] = jnp.zeros(out.shape, BF16)
        for f0, dprime, row0, length in p.att_seg:
            out[dprime, row0 : row0 + length, :] = flat[f0 : f0 + length, :].astype(BF16)
        for f0, dprime, row0, length in p.gain_seg:
            out[dprime, row0 : row0 + length, :] = v_ref[
                9 + f0 - G0 : 9 + f0 - G0 + length, :
            ].astype(BF16)
        pos = 0
        for _, _, dprime, row0, length in p.wd_seg:
            size = up(length, 16)
            out[dprime, row0 : row0 + size, :] = w_ref[pos : pos + size, :]
            pos += size

    return pl.pallas_call(
        kernel,
        name="store_attention_grads",
        out_shape=jax.ShapeDtypeStruct((p.dp, p.RS, 128), BF16),
        in_specs=[vspec()] * 4,
        out_specs=vspec(),
        scratch_shapes=[VM((ATT + 7, 128), F32)],
        compiler_params=params(),
        cost_estimate=cost(0, 20e6),
    )(dwqkv, dwo, vec, wdsp)


def load_mlp_weights(p, scal, a_tab, n_tab, pieces, rel):
    width = p.NB * 128
    count = p.ctx * p.dp

    def kernel(s_ref, a_ref, n_ref, piece_ref, rel_ref, wgu, wd, tall, stage):
        d = s_ref[0]

        def clear(j, carry):
            tall[pl.ds(pl.multiple_of(j * 128, 128), 128), :] = jnp.zeros((128, 128), BF16)
            return carry

        lax.fori_loop(0, p.TR // 128, clear, 0)

        def one_piece(j, carry):
            base = a_ref[j]

            def one_chunk(k, inner):
                at = pl.multiple_of(base + k * CH, 16)
                frm = pl.multiple_of(k * CH, CH)
                tall[pl.ds(at, CH), :] = tall[pl.ds(at, CH), :] + piece_ref[j, pl.ds(frm, CH), :]
                return inner

            return lax.fori_loop(0, n_ref[j], one_chunk, carry)

        lax.fori_loop(0, count, one_piece, 0)
        for dest, t0, dprime, row0, length in p.wd_seg:

            @pl.when(d == dest)
            def _():
                size = up(length, 16)
                tall[t0 : t0 + size, :] = (
                    tall[t0 : t0 + size, :] + rel_ref[d ^ dprime, row0 : row0 + size, :]
                )

        per = 128 * p.NB

        def gu(j, carry):
            at = pl.multiple_of(j * per, 128)
            stage[0:per, :] = tall[pl.ds(at, per), :].astype(F32)
            row = pl.multiple_of(j * 128, 128)
            for s in range(p.NB):
                wgu[pl.ds(row, 128), 128 * s : 128 * s + 128] = stage[
                    pl.ds(s, 128, stride=p.NB), :
                ].astype(BF16)
            return carry

        lax.fori_loop(0, 2 * D // 128, gu, 0)

        def down(j, carry):
            at = pl.multiple_of(p.TG + j * 896, 128)
            stage[0:896, :] = tall[pl.ds(at, 896), :].astype(F32)
            row = pl.multiple_of(j * 128, 128)
            for s in range(7):
                wd[pl.ds(row, 128), 128 * s : 128 * s + 128] = stage[
                    pl.ds(s, 128, stride=7), :
                ].astype(BF16)
            return carry

        lax.fori_loop(0, p.NB, down, 0)

    return pl.pallas_call(
        kernel,
        name="load_mlp_weights",
        out_shape=(
            jax.ShapeDtypeStruct((2 * D, width), BF16),
            jax.ShapeDtypeStruct((width, D), BF16),
        ),
        in_specs=[sspec()] * 3 + [vspec()] * 2,
        out_specs=(vspec(),) * 2,
        scratch_shapes=[
            VM((p.TR + p.U, 128), BF16),
            VM((max(128 * p.NB, 896), 128), F32),
        ],
        compiler_params=params(),
        cost_estimate=cost(0, 40e6),
    )(scal, a_tab, n_tab, pieces, rel)


def store_mlp_grads(p, scal, a_tab, dwgu, dwd):
    count = p.ctx * p.dp
    per = 128 * p.NB
    sizes = [up(s[4], 16) for s in p.wd_seg]
    total = max(sum(sizes), 16)
    steps_g = 2 * D // 128
    steps = steps_g + p.NB

    def kernel(s_ref, a_ref, g_ref, w_ref, pieces, wdsp, tall, stage, sem):
        d = s_ref[0]
        step = pl.program_id(0)

        @pl.when(step == 0)
        def _():
            tall[p.TR : p.TR + p.U, :] = jnp.zeros((p.U, 128), BF16)

        @pl.when(step < steps_g)
        def _():
            for s in range(p.NB):
                stage[pl.ds(s, 128, stride=p.NB), :] = g_ref[:, 128 * s : 128 * s + 128]
            at = pl.multiple_of(step * per, 128)
            tall[pl.ds(at, per), :] = stage[0:per, :].astype(BF16)

        @pl.when(step >= steps_g)
        def _():
            for s in range(7):
                stage[pl.ds(s, 128, stride=7), :] = w_ref[:, 128 * s : 128 * s + 128]
            at = pl.multiple_of(p.TG + (step - steps_g) * 896, 128)
            tall[pl.ds(at, 896), :] = stage[0:896, :].astype(BF16)

        @pl.when(step == steps - 1)
        def _():
            def copy_of(j):
                at = pl.multiple_of(a_ref[j], 16)
                return pltpu.make_async_copy(tall.at[pl.ds(at, p.U), :], pieces.at[j], sem.at[j])

            def start(j, carry):
                copy_of(j).start()
                return carry

            def wait(j, carry):
                copy_of(j).wait()
                return carry

            lax.fori_loop(0, count, start, 0)
            wdsp[...] = jnp.zeros(wdsp.shape, BF16)
            pos = 0
            for (dest, t0, _, _, _), size in zip(p.wd_seg, sizes):

                @pl.when(d == dest)
                def _():
                    wdsp[pos : pos + size, :] = tall[t0 : t0 + size, :]

                pos += size
            lax.fori_loop(0, count, wait, 0)

    return pl.pallas_call(
        kernel,
        name="store_mlp_grads",
        grid=(steps,),
        out_shape=(
            jax.ShapeDtypeStruct((count, p.U, 128), BF16),
            jax.ShapeDtypeStruct((total, 128), BF16),
        ),
        in_specs=[
            sspec(),
            sspec(),
            pl.BlockSpec((128, per), lambda i: (jnp.minimum(i, steps_g - 1), 0)),
            pl.BlockSpec((128, D), lambda i: (jnp.maximum(i - steps_g, 0), 0)),
        ],
        out_specs=(aspec(), pl.BlockSpec((total, 128), lambda i: (0, 0))),
        scratch_shapes=[
            VM((p.TR + p.U, 128), BF16),
            VM((max(per, 896), 128), F32),
            pltpu.SemaphoreType.DMA((count,)),
        ],
        compiler_params=params(),
        cost_estimate=cost(0, 40e6),
    )(scal, a_tab, dwgu, dwd)


def lane_low(shape):
    return lax.broadcasted_iota(jnp.int32, shape, len(shape) - 1) < HEAD


def half_variants(x, out):
    xf = x.astype(F32)
    rolled = pltpu.roll(xf, HEAD, 1)
    low = lane_low(xf.shape)
    out[0] = jnp.where(low, xf, 0.0).astype(BF16)
    out[1] = jnp.where(low, 0.0, rolled).astype(BF16)
    out[2] = jnp.where(low, rolled, 0.0).astype(BF16)
    out[3] = jnp.where(low, 0.0, xf).astype(BF16)


def half_variants_t(xt, out):
    xf = xt.astype(F32)
    swapped = jnp.concatenate([xf[HEAD:], xf[:HEAD]], axis=0)
    low = lax.broadcasted_iota(jnp.int32, xf.shape, 0) < HEAD
    out[0] = jnp.where(low, xf, 0.0).astype(BF16)
    out[1] = jnp.where(low, 0.0, swapped).astype(BF16)
    out[2] = jnp.where(low, swapped, 0.0).astype(BF16)
    out[3] = jnp.where(low, 0.0, xf).astype(BF16)


def dot(a, b):
    return jnp.dot(a, b, preferred_element_type=F32)


def attention_forward(q_t, keys, values_t, bias):
    toks, length = q_t.shape[1], keys.shape[0]
    groups = HEADS // KV_HEADS

    def kernel(q_ref, k_ref, v_ref, b_ref, o_ref, l_ref, kvar, vvar):
        blk = pl.program_id(0)

        @pl.when(blk == 0)
        def _():
            half_variants(k_ref[...], kvar)
            half_variants_t(v_ref[...], vvar)

        acc = None
        for half in range(2):
            var = 2 * ((2 * blk + half) // groups) + half
            s = dot(kvar[var], q_ref[...]) + b_ref[...]
            peak = jnp.max(s, axis=0, keepdims=True)
            e = jnp.exp(s - peak)
            total = jnp.sum(e, axis=0, keepdims=True)
            probs = (e * (1.0 / total)).astype(BF16)
            part = dot(vvar[var], probs)
            acc = part if acc is None else acc + part
            l_ref[0, half : half + 1, :] = peak + jnp.log(total)
        o_ref[...] = acc.T

    return pl.pallas_call(
        kernel,
        name="attention_forward",
        grid=(7,),
        out_shape=(
            jax.ShapeDtypeStruct((toks, D), F32),
            jax.ShapeDtypeStruct((7, 8, toks), F32),
        ),
        in_specs=[pl.BlockSpec((128, toks), lambda i: (i, 0)), vspec(), vspec(), vspec()],
        out_specs=(
            pl.BlockSpec((toks, 128), lambda i: (0, i)),
            pl.BlockSpec((1, 8, toks), lambda i: (i, 0, 0)),
        ),
        scratch_shapes=[VM((4, length, 128), BF16), VM((4, 128, length), BF16)],
        compiler_params=params(),
        cost_estimate=cost(8 * 14 * 256 * 2048 * 128, 4e6),
    )(q_t, keys, values_t, bias)


def attention_backward(q_t, q, do_t, do, keys, keys_t, values, bias, lse, delta):
    toks, length = q_t.shape[1], keys.shape[0]
    groups = HEADS // KV_HEADS

    def kernel(
        qt_ref, q_ref, dot_ref, do_ref, k_ref, kt_ref, v_ref, b_ref, l_ref, d_ref,
        dq_ref, dk_ref, dv_ref, kvar, ktvar, vvar, dk_acc, dv_acc,
    ):
        blk = pl.program_id(0)

        @pl.when(blk == 0)
        def _():
            half_variants(k_ref[...], kvar)
            half_variants(v_ref[...], vvar)
            half_variants_t(kt_ref[...], ktvar)
            dk_acc[...] = jnp.zeros(dk_acc.shape, F32)
            dv_acc[...] = jnp.zeros(dv_acc.shape, F32)

        low = lane_low((toks, 128))
        acc = None
        for half in range(2):
            group = (2 * blk + half) // groups
            var = 2 * group + half
            keep = low if half == 0 else jnp.logical_not(low)
            q_half = jnp.where(keep, q_ref[...].astype(F32), 0.0).astype(BF16)
            do_half = jnp.where(keep, do_ref[...].astype(F32), 0.0).astype(BF16)
            s = dot(kvar[var], qt_ref[...]) + b_ref[...]
            prob = jnp.exp(s - l_ref[0, half : half + 1, :])
            dv_acc[group] += dot(prob.astype(BF16), do_half)
            dp = dot(vvar[var], dot_ref[...])
            ds = (prob * (dp - d_ref[0, half : half + 1, :])).astype(BF16)
            dk_acc[group] += dot(ds, q_half)
            part = dot(ktvar[var], ds)
            acc = part if acc is None else acc + part
        dq_ref[...] = acc.T

        @pl.when(blk == 6)
        def _():
            lowk = lane_low((length, 128))
            for a_ref, o_ref in ((dk_acc, dk_ref), (dv_acc, dv_ref)):
                one, two = a_ref[0], a_ref[1]
                one = one + pltpu.roll(one, HEAD, 1)
                two = two + pltpu.roll(two, HEAD, 1)
                o_ref[...] = jnp.where(lowk, one, two)

    return pl.pallas_call(
        kernel,
        name="attention_backward",
        grid=(7,),
        out_shape=(
            jax.ShapeDtypeStruct((toks, D), F32),
            jax.ShapeDtypeStruct((length, 128), F32),
            jax.ShapeDtypeStruct((length, 128), F32),
        ),
        in_specs=[
            pl.BlockSpec((128, toks), lambda i: (i, 0)),
            pl.BlockSpec((toks, 128), lambda i: (0, i)),
            pl.BlockSpec((128, toks), lambda i: (i, 0)),
            pl.BlockSpec((toks, 128), lambda i: (0, i)),
            vspec(), vspec(), vspec(), vspec(),
            pl.BlockSpec((1, 8, toks), lambda i: (i, 0, 0)),
            pl.BlockSpec((1, 8, toks), lambda i: (i, 0, 0)),
        ],
        out_specs=(
            pl.BlockSpec((toks, 128), lambda i: (0, i)),
            pl.BlockSpec((length, 128), lambda i: (0, 0)),
            pl.BlockSpec((length, 128), lambda i: (0, 0)),
        ),
        scratch_shapes=[
            VM((4, length, 128), BF16),
            VM((4, 128, length), BF16),
            VM((4, length, 128), BF16),
            VM((2, length, 128), F32),
            VM((2, length, 128), F32),
        ],
        compiler_params=params(),
        cost_estimate=cost(20 * 14 * 256 * 2048 * 128, 8e6),
    )(q_t, q, do_t, do, keys, keys_t, values, bias, lse, delta)


def rms_scale(values):
    return lax.rsqrt(jnp.mean(values * values, axis=-1, keepdims=True) + RMS_EPS)


def rms_back(values, scale_vals, gain, grad_out):
    unit_vals = values * scale_vals
    gain_grad = jnp.sum(grad_out * unit_vals, axis=0)
    grad_unit = grad_out * gain
    inner = jnp.mean(grad_unit * unit_vals, axis=-1, keepdims=True)
    return (scale_vals * (grad_unit - unit_vals * inner), gain_grad)


def rope_tables(positions):
    half_dim = HEAD // 2
    inverse = ROPE_BASE ** (-(jnp.arange(half_dim, dtype=F32) * 2.0 / HEAD))
    angles = positions.astype(F32)[:, None] * inverse[None, :]
    return jnp.cos(angles)[:, None, :], jnp.sin(angles)[:, None, :]


def rotate(values, tables, sign):
    cosine, sine = tables
    sine = sine * sign
    first = values[..., : HEAD // 2]
    second = values[..., HEAD // 2 :]
    return jnp.concatenate(
        [first * cosine - second * sine, second * cosine + first * sine], axis=-1
    )


def ancestor_bits(parents):
    tree_count, seg_count = parents.shape
    current = jnp.broadcast_to(
        jnp.arange(seg_count, dtype=jnp.int32)[None, :], (tree_count, seg_count)
    )
    bits = jnp.zeros((tree_count, seg_count), jnp.int32)
    hot = jnp.arange(seg_count, dtype=jnp.int32)
    for _ in range(seg_count):
        bits = jnp.bitwise_or(bits, jnp.left_shift(jnp.ones_like(current), current))
        pick = current[:, :, None] == hot[None, None, :]
        current = jnp.sum(jnp.where(pick, parents[:, None, :], 0), axis=2)
    return bits


def swap(x, axis, size, mask):
    return lax.ppermute(x, axis, [(i, i ^ mask) for i in range(size)])


def body(p, inputs, cotangent, parents, lengths, positions, master, moment_one, moment_two):
    toks = inputs.shape[0]
    dp, ctx, n, U = p.dp, p.ctx, p.n, p.U
    d, c = lax.axis_index("dp"), lax.axis_index("ctx")
    core = jnp.bitwise_and(c, 1)
    scal = d.reshape(1).astype(jnp.int32)
    owner = d * ctx + c

    def pick(table, i):
        return lax.dynamic_index_in_dim(jnp.asarray(table), i, 0, keepdims=False)

    def dyn(x, i):
        return lax.dynamic_index_in_dim(x, i, 0, keepdims=False)

    a_tab, n_tab = pick(p.aT, d), pick(p.nT, d)
    pieces = spread_rows(pick(p.fwd, owner), master).reshape(dp, U, 128)
    got = [pieces[0]] + [swap(pieces[q], "dp", dp, q) for q in range(1, dp)]
    gathered = jnp.stack(got)
    late = jnp.concatenate(
        [dyn(gathered, d ^ s)[U - p.ns[s] :] for s in range(dp) if p.ns[s]], axis=0
    )
    late_all = lax.all_gather(late, "ctx", axis=0)
    gathered, late_all = lax.optimization_barrier((gathered, late_all))
    mlp_pieces = lax.all_gather(gathered, "ctx", axis=0)
    sp_own = jnp.concatenate(
        [late_all[cc, p.lo[s] : p.lo[s] + p.ns[s]] for (_, s, cc, _, _) in p.so], axis=0
    )
    half_rows = p.RS // 2
    sp_half = lax.dynamic_slice_in_dim(sp_own, core * half_rows, half_rows, 0)
    mine = jnp.stack([swap(sp_half, "dp", dp, q) for q in range(1, dp)])
    theirs = swap(mine, "ctx", ctx, 1)
    first = jnp.where(core == 0, mine, theirs)
    second_half = jnp.where(core == 0, theirs, mine)
    rel = jnp.concatenate([sp_own[None], jnp.concatenate([first, second_half], axis=1)], axis=0)
    w_qkv, w_out, vec = load_attention_weights(p, scal, rel)
    bias_qkv = vec[0:9].reshape(1152)
    norm_one, norm_two = vec[9:16].reshape(D), vec[16:23].reshape(D)

    per_tree = TREE_LEN // toks
    z_count = per_tree // 2
    bits_all = ancestor_bits(parents)
    ends_all = jnp.cumsum(lengths, axis=1)
    tree = c // per_tree
    ends, bits = dyn(ends_all, tree), dyn(bits_all, tree)

    def seg_of(index):
        return jnp.sum((index[:, None] >= ends[None, :]).astype(jnp.int32), axis=1)

    tok_iota = jnp.arange(toks, dtype=jnp.int32)
    q_idx = (c % per_tree) * toks + tok_iota
    k_idx = jnp.concatenate(
        [
            ((c ^ (2 * q) ^ r) % per_tree) * toks + tok_iota
            for r in range(2)
            for q in range(z_count)
        ]
    )
    q_seg, k_seg = seg_of(q_idx), seg_of(k_idx)
    seg_iota = jnp.arange(ends.shape[0], dtype=jnp.int32)
    q_bits = jnp.sum(jnp.where(q_seg[:, None] == seg_iota[None, :], bits[None, :], 0), axis=1)
    allowed = (jnp.right_shift(q_bits[None, :], k_seg[:, None]) & 1 == 1) & (
        k_idx[:, None] <= q_idx[None, :]
    )
    bias = jnp.where(allowed, 0.0, NEG_FILL).astype(F32)
    tables = rope_tables(positions)
    cots = jnp.concatenate(
        [cotangent] + [swap(cotangent, "dp", dp, q) for q in range(1, dp)], axis=0
    )

    x = inputs.astype(F32)
    scale_one = rms_scale(x)
    normed = (x * scale_one * norm_one).astype(BF16)
    qkv = dot(normed, w_qkv) + bias_qkv
    query = rotate(qkv[:, :D].reshape(toks, HEADS, HEAD), tables, 1.0).reshape(toks, D)
    query = query.astype(BF16) * jnp.asarray(HEAD**-0.5, BF16)
    key = rotate(qkv[:, D : D + 128].reshape(toks, KV_HEADS, HEAD), tables, 1.0)
    kv = jnp.concatenate(
        [key.reshape(toks, 128).astype(BF16), qkv[:, D + 128 :].astype(BF16)], axis=1
    )
    kv_own = jnp.stack([kv] + [swap(kv, "ctx", ctx, 2 * q) for q in range(1, z_count)])
    kv_all = jnp.concatenate([kv_own, swap(kv_own, "ctx", ctx, 1)]).reshape(TREE_LEN, 256)
    keys, values = kv_all[:, :128], kv_all[:, 128:]
    q_t = query.T
    attended, lse = attention_forward(q_t, keys, values.T, bias)
    attended_b = attended.astype(BF16)
    middle = x + dot(attended_b, w_out)
    scale_two = rms_scale(middle)
    second = (middle * scale_two * norm_two).astype(BF16)

    w_gu, w_down = load_mlp_weights(
        p, scal, a_tab, n_tab, mlp_pieces.reshape(ctx * dp, U, 128), rel
    )
    w_gate, w_up = w_gu[:D], w_gu[D:]
    seconds = jnp.concatenate(
        [second] + [swap(second, "dp", dp, q) for q in range(1, dp)], axis=0
    )

    def back_to_owner(part):
        blocks = part.reshape(dp, toks, D)
        total = blocks[0]
        for q in range(1, dp):
            total = total + swap(blocks[q].astype(BF16), "dp", dp, q).astype(F32)
        return total

    gate = dot(seconds, w_gate)
    up_act = dot(seconds, w_up)
    gate_sig = jax.nn.sigmoid(gate)
    hidden = (gate * gate_sig * up_act).astype(BF16)
    d_hidden = jnp.einsum("td,fd->tf", cots, w_down, preferred_element_type=F32)
    d_gate = (d_hidden * up_act * gate_sig * (1.0 + gate * (1.0 - gate_sig))).astype(BF16)
    d_up = (d_hidden * gate * gate_sig).astype(BF16)
    d_second_part = jnp.einsum(
        "tf,df->td", d_gate, w_gate, preferred_element_type=F32
    ) + jnp.einsum("tf,df->td", d_up, w_up, preferred_element_type=F32)
    d_second = back_to_owner(d_second_part)
    activations = (middle + back_to_owner(dot(hidden, w_down))).astype(BF16)
    dw_gate = jnp.einsum("td,tf->df", seconds, d_gate, preferred_element_type=F32)
    dw_up = jnp.einsum("td,tf->df", seconds, d_up, preferred_element_type=F32)
    dw_down = jnp.einsum("tf,td->fd", hidden, cots, preferred_element_type=F32)
    grad_pieces, wd_special = store_mlp_grads(
        p, scal, a_tab, jnp.concatenate([dw_gate, dw_up], axis=0), dw_down
    )
    own_pieces = lax.psum_scatter(
        grad_pieces.reshape(ctx, dp, U, 128), "ctx", scatter_dimension=0, tiled=False
    )

    middle_norm_grad, gain_two_grad = rms_back(middle, scale_two, norm_two, d_second)
    middle_grad = cotangent.astype(F32) + middle_norm_grad
    branch = middle_grad.astype(BF16)
    dw_out = jnp.einsum("th,td->hd", attended_b, branch, preferred_element_type=F32)
    d_out = jnp.einsum("td,hd->th", branch, w_out, preferred_element_type=F32).astype(BF16)
    delta = jnp.sum((d_out.astype(F32) * attended).reshape(toks, HEADS, HEAD), axis=-1)
    delta = jnp.pad(delta.T.reshape(7, 2, toks), ((0, 0), (0, 6), (0, 0)))
    d_query, d_key, d_value = attention_backward(
        q_t, query, d_out.T, d_out, keys, keys.T, values, bias, lse, delta
    )
    d_kv = jnp.concatenate([d_key, d_value], axis=1).reshape(2, z_count, toks, 256)
    d_kv = d_kv[0] + swap(d_kv[1].astype(BF16), "ctx", ctx, 1).astype(F32)
    kv_grad = d_kv[0]
    for q in range(1, z_count):
        kv_grad = kv_grad + swap(d_kv[q].astype(BF16), "ctx", ctx, 2 * q).astype(F32)
    dq_pre = rotate((d_query * HEAD**-0.5).reshape(toks, HEADS, HEAD), tables, -1.0)
    dk_pre = rotate(
        kv_grad[:, :128].astype(BF16).astype(F32).reshape(toks, KV_HEADS, HEAD), tables, -1.0
    )
    d_qkv = jnp.concatenate(
        [dq_pre.reshape(toks, D), dk_pre.reshape(toks, 128), kv_grad[:, 128:]], axis=1
    ).astype(BF16)
    dw_qkv = jnp.einsum("td,th->dh", normed, d_qkv, preferred_element_type=F32)
    db_qkv = jnp.sum(d_qkv.astype(F32), axis=0)
    d_normed = jnp.einsum("th,dh->td", d_qkv, w_qkv, preferred_element_type=F32)
    input_norm_grad, gain_one_grad = rms_back(x, scale_one, norm_one, d_normed)
    input_grad = middle_grad + input_norm_grad

    vec_grad = jnp.concatenate(
        [db_qkv, gain_one_grad, gain_two_grad, jnp.zeros((128,), F32)]
    ).reshape(24, 128)
    sp_grad = store_attention_grads(p, dw_qkv, dw_out, vec_grad, wd_special)
    keep = lax.dynamic_slice_in_dim(sp_grad, core * half_rows, half_rows, 1)
    give = lax.dynamic_slice_in_dim(sp_grad, (1 - core) * half_rows, half_rows, 1)
    pair = (keep.astype(F32) + swap(give, "ctx", ctx, 1).astype(F32)).astype(BF16)
    chunk = dyn(pair, d).astype(F32)
    for q in range(1, dp):
        chunk = chunk + swap(dyn(pair, d ^ q), "dp", dp, q).astype(F32)
    chunk = lax.dynamic_update_slice_in_dim(
        jnp.zeros((p.RS, 128), BF16), chunk.astype(BF16), core * half_rows, 0
    )
    offset_of = {(s, cc): off for (_, s, cc, _, off) in p.so}
    rows = []
    for cc in range(ctx):
        for s in range(dp):
            if p.ns[s]:
                if (s, cc) in offset_of:
                    off = offset_of[(s, cc)]
                    rows.append(chunk[off : off + p.ns[s]])
                else:
                    rows.append(jnp.zeros((p.ns[s], 128), BF16))
    late_in, own_pieces = lax.optimization_barrier(
        (jnp.concatenate(rows, axis=0).reshape(ctx, p.NL, 128), own_pieces)
    )
    late_grad = lax.psum_scatter(
        late_in,
        "ctx",
        scatter_dimension=0,
        tiled=False,
    )
    late_grad = jnp.pad(late_grad, ((0, p.nsm), (0, 0)))

    def late_for(q):
        return lax.dynamic_slice_in_dim(late_grad, pick(p.lo.astype(np.int32), d ^ q), p.nsm, 0)

    parts = [dyn(own_pieces, jnp.int32(0))]
    parts += [swap(own_pieces[q], "dp", dp, q) for q in range(1, dp)]
    parts += [late_for(0)] + [swap(late_for(q), "dp", dp, q) for q in range(1, dp)]
    own_grad = collect_rows(pick(p.back_padded, owner), parts, n)
    own_grad = own_grad * (toks * dp * ctx) ** (-0.5)
    new_one = BETA_ONE * moment_one + (1.0 - BETA_ONE) * own_grad
    new_two = BETA_TWO * moment_two + (1.0 - BETA_TWO) * own_grad * own_grad
    corrected_one = new_one / (1.0 - BETA_ONE**STEP)
    corrected_two = new_two / (1.0 - BETA_TWO**STEP)
    new_master = master - LEARN_RATE * (
        corrected_one / (jnp.sqrt(corrected_two) + ADAM_EPS) + DECAY_RATE * master
    )
    return (activations, input_grad, new_master, new_one, new_two)


def solution(mesh):
    dp, ctx = mesh.shape["dp"], mesh.shape["ctx"]

    def run(inputs, cotangent, parents, lengths, positions, master, moment_one, moment_two):
        n = master.shape[0] // (dp * ctx)
        p = make(dp, ctx, n)
        extra = up(n, 16) - n
        p.back_padded = np.pad(p.back, ((0, 0), (0, extra)), constant_values=p.zero_back)
        row = P(("dp", "ctx"), None)
        step = jax.shard_map(
            functools.partial(body, p),
            mesh=mesh,
            in_specs=(row, row, P("dp", None), P("dp", None), P(("dp", "ctx")), row, row, row),
            out_specs=(row,) * 5,
            check_vma=False,
        )
        return step(
            inputs, cotangent, parents, lengths, positions, master, moment_one, moment_two
        )

    return run
```

```python
import functools
import math

import jax
import jax.numpy as jnp
import numpy as np
from jax import lax
from jax.experimental import pallas as pl
from jax.experimental.pallas import tpu as pltpu
from jax.sharding import PartitionSpec as P

D = 896
HEADS = 14
KV_HEADS = 2
HEAD = 64
FF = 4864
TREE_LEN = 2048
STEP = 10
RMS_EPS = 1e-06
ROPE_BASE = 1000000.0
BETA_ONE = 0.9
BETA_TWO = 0.95
ADAM_EPS = 1e-08
LEARN_RATE = 0.01
DECAY_RATE = 0.1
NEG_FILL = -1e30
F32 = jnp.float32
BF16 = jnp.bfloat16


ATT, WG0, WD0, G0, END = 14345, 14345, 82441, 116489, 116503
NFB = 38
CH = 32


def up(v, m):
    return -(-v // m) * m


class Plan:
    pass


def make(dp, ctx, n):
    p = Plan()
    count = dp * ctx
    p.dp, p.ctx, p.n, p.nz = dp, ctx, n, ctx // 2
    p.NB = NB = -(-NFB // dp)
    p.TG = 2 * D * NB
    p.TR = p.TG + NB * 896
    r = np.arange(count * n)
    own = r // n
    straddle_end = (WD0 // n + 1) * n if WD0 % n else WD0
    class_a = (r < ATT) | ((r >= G0) & (r < END))
    class_b = (r >= WD0) & (r < straddle_end)
    special = class_a | class_b
    gate_up = (r >= WG0) & (r < WD0)
    b = np.where(gate_up, (r - WG0) % NFB, (r - WD0) // 896)
    rank, slot = b % dp, b // dp
    t = np.where(
        gate_up, ((r - WG0) // NFB) * NB + slot, p.TG + slot * 896 + (r - WD0) % 896
    )
    mlp = ~special & (r < END)
    cnt_a = np.bincount(own[class_a], minlength=count)
    cnt_b = np.bincount(own[class_b], minlength=count)
    assert not ((cnt_a > 0) & (cnt_b > 0)).any()
    p.nsA = [up(-(-int(m) // dp), 16) for m in cnt_a.reshape(dp, ctx).max(1)]
    p.nsB = [up(-(-int(m) // dp), 16) for m in cnt_b.reshape(dp, ctx).max(1)]
    p.nsm = max(p.nsA + p.nsB)
    a = np.zeros((count, dp), np.int64)
    ln = np.zeros((count, dp), np.int64)
    for o in range(count):
        rows = np.arange(o * n, (o + 1) * n)
        for d in range(dp):
            mine = rows[mlp[rows] & (rank[rows] == d)]
            if len(mine):
                a[o, d] = t[mine].min() // 16 * 16
                ln[o, d] = up(t[mine].max() + 1 - a[o, d], CH)
    ns_of = [
        p.nsA[o // ctx] if cnt_a[o] else (p.nsB[o // ctx] if cnt_b[o] else 0)
        for o in range(count)
    ]
    p.U = U = up(max(int(ln[o].max()) + ns_of[o] for o in range(count)), 32)
    p.fwd = np.full((count, dp * U), n, np.int32)
    padded = up(n, 16)
    p.back = np.full((count, padded), dp * U, np.int32)
    p.late = np.zeros((count, 2), np.int32)
    for o in range(count):
        home = o // ctx
        rows = np.arange(o * n, (o + 1) * n)
        k = np.nonzero(mlp[rows])[0]
        q = rank[rows[k]] ^ home
        pos = t[rows[k]] - a[o, rank[rows[k]]]
        p.fwd[o, q * U + pos] = k
        p.back[o, k] = q * U + pos
        k = np.nonzero(special[rows])[0]
        if len(k):
            assert k[-1] - k[0] + 1 == len(k)
            s = np.arange(len(k))
            p.fwd[o, (s // ns_of[o] ^ home) * U + U - ns_of[o] + s % ns_of[o]] = k
            p.late[o] = k[0], ns_of[o]
    p.aT = np.zeros((dp, ctx, dp), np.int32)
    p.nT = np.zeros((dp, ctx, dp), np.int32)
    for d in range(dp):
        for c in range(ctx):
            for q in range(dp):
                p.aT[d, c, q] = a[(d ^ q) * ctx + c, d]
                p.nT[d, c, q] = ln[(d ^ q) * ctx + c, d] // CH
    p.aT, p.nT = p.aT.reshape(dp, -1), p.nT.reshape(dp, -1)

    has_a = (cnt_a > 0).reshape(dp, p.nz, 2)
    p.pairs = [(s, z) for s in range(dp) for z in range(p.nz) if has_a[s, z].any()]
    p.offA, off = {}, 0
    for s, z in p.pairs:
        p.offA[s, z] = off
        off += p.nsA[s]
    p.RA = off
    p.loA, off = {}, 0
    for s in range(dp):
        if p.nsA[s]:
            p.loA[s] = off
            off += p.nsA[s]
    p.NLA = off

    def runs(o, first, length, ns, base):
        out, s = [], 0
        while s < length:
            e = min((s // ns + 1) * ns, length)
            out.append((int(o * n + first + s), s // ns, base + s % ns, e - s))
            s = e
        return out

    p.att_seg, p.gain_seg, p.wd_seg, p.ownB = [], [], [], []
    for o in range(count):
        s, c = o // ctx, o % ctx
        if cnt_a[o]:
            for f0, dd, row, length in runs(o, int(p.late[o][0]), int(cnt_a[o]), p.nsA[s], p.offA[s, c // 2]):
                (p.att_seg if f0 < ATT else p.gain_seg).append((f0, c & 1, dd, row, length))
        if cnt_b[o]:
            p.ownB.append((s, c))
            for f0, dd, row, length in runs(o, int(p.late[o][0]), int(cnt_b[o]), p.nsB[s], 0):
                x = f0
                while x < f0 + length:
                    blk = (x - WD0) // 896
                    e = min(f0 + length, WD0 + (blk + 1) * 896)
                    p.wd_seg.append(
                        (blk % dp, p.TG + (blk // dp) * 896 + (x - WD0) % 896, dd, row + x - f0, e - x)
                    )
                    x = e
    assert len(p.ownB) <= 1
    p.RB = max(p.nsB) or 16
    p.msg, p.offM = [], np.zeros((p.nz, dp), np.int32)
    p.M = 16
    for z in range(p.nz):
        parts, off = [], 0
        for s in range(dp):
            if (s, z) in p.offA:
                p.offM[z, s] = off
                parts.append(("A", p.offA[s, z], p.nsA[s]))
                off += p.nsA[s]
            if p.ownB and p.ownB[0][0] == s and p.ownB[0][1] // 2 == z:
                assert (s, z) not in p.offA
                p.offM[z, s] = off
                parts.append(("B", 0, p.nsB[s]))
                off += p.nsB[s]
        p.msg.append(parts)
        p.M = max(p.M, off)
    return p


VM = pltpu.VMEM


def vspec():
    return pl.BlockSpec(memory_space=pltpu.VMEM)


def sspec():
    return pl.BlockSpec(memory_space=pltpu.SMEM)


def aspec():
    return pl.BlockSpec(memory_space=pl.ANY)


def cost(flops, nbytes):
    return pl.CostEstimate(flops=int(flops), bytes_accessed=int(nbytes), transcendentals=0)


def params():
    return pltpu.CompilerParams(vmem_limit_bytes=60 * 1024 * 1024)


def row_loop(count, idx_ref, src_ref, dst_ref):
    def step(j, carry):
        for u in range(16):
            row = j * 16 + u
            dst_ref[pl.ds(row, 1), :] = src_ref[pl.ds(idx_ref[row], 1), :]
        return carry

    lax.fori_loop(0, count // 16, step, 0)


def spread_rows(table, shard):
    n, total = shard.shape[0], table.shape[0]

    def kernel(idx_ref, x_ref, o_ref, xs, os):
        low = n // 8 * 8
        xs[low : low + 16, :] = jnp.zeros((16, 128), F32)
        xs[0:n, :] = x_ref[...]
        row_loop(total, idx_ref, xs, os)
        o_ref[...] = os[...].astype(BF16)

    return pl.pallas_call(
        kernel,
        name="spread_rows",
        out_shape=jax.ShapeDtypeStruct((total, 128), BF16),
        in_specs=[sspec(), vspec()],
        out_specs=vspec(),
        scratch_shapes=[VM((n // 8 * 8 + 16, 128), F32), VM((total, 128), F32)],
        compiler_params=params(),
        cost_estimate=cost(0, total * 4096),
    )(table, shard)


def collect_rows(table, parts, n):
    total = sum(p.shape[0] for p in parts)
    padded = table.shape[0]

    def kernel(idx_ref, *refs):
        ins, o_ref, xs, os = refs[: len(parts)], refs[-3], refs[-2], refs[-1]
        base = 0
        for ref in ins:
            size = ref.shape[0]
            xs[base : base + size, :] = ref[...].astype(F32)
            base += size
        xs[total : total + 8, :] = jnp.zeros((8, 128), F32)
        row_loop(padded, idx_ref, xs, os)
        o_ref[...] = os[0:n, :]

    return pl.pallas_call(
        kernel,
        name="collect_rows",
        out_shape=jax.ShapeDtypeStruct((n, 128), F32),
        in_specs=[sspec()] + [vspec()] * len(parts),
        out_specs=vspec(),
        scratch_shapes=[VM((total + 8, 128), F32), VM((padded, 128), F32)],
        compiler_params=params(),
        cost_estimate=cost(0, padded * 4096),
    )(table, *parts)


def load_mlp_weights(p, scal, a_tab, n_tab, pieces, rel):
    width = p.NB * 128
    count = p.ctx * p.dp

    def kernel(s_ref, a_ref, n_ref, piece_ref, rel_ref, wgu, wd, tall, stage):
        d = s_ref[0]

        def clear(j, carry):
            tall[pl.ds(pl.multiple_of(j * 128, 128), 128), :] = jnp.zeros((128, 128), BF16)
            return carry

        lax.fori_loop(0, p.TR // 128, clear, 0)

        def one_piece(j, carry):
            base = a_ref[j]

            many = n_ref[j] // 8

            def chunk_of(size, start):
                def one_chunk(k, inner):
                    frm = pl.multiple_of(start + k * size, CH)
                    at = pl.multiple_of(base + frm, 16)
                    tall[pl.ds(at, size), :] = (
                        tall[pl.ds(at, size), :] + piece_ref[j, pl.ds(frm, size), :]
                    )
                    return inner

                return one_chunk

            lax.fori_loop(0, many, chunk_of(8 * CH, 0), 0)
            lax.fori_loop(0, n_ref[j] - many * 8, chunk_of(CH, many * 8 * CH), 0)
            return carry

        lax.fori_loop(0, count, one_piece, 0)
        for dest, t0, dprime, row0, length in p.wd_seg:

            @pl.when(d == dest)
            def _():
                size = up(length, 16)
                tall[t0 : t0 + size, :] = (
                    tall[t0 : t0 + size, :] + rel_ref[d ^ dprime, row0 : row0 + size, :]
                )

        per = 128 * p.NB

        def gu(j, carry):
            at = pl.multiple_of(j * per, 128)
            stage[0:per, :] = tall[pl.ds(at, per), :].astype(F32)
            row = pl.multiple_of(j * 128, 128)
            for s in range(p.NB):
                wgu[pl.ds(row, 128), 128 * s : 128 * s + 128] = stage[
                    pl.ds(s, 128, stride=p.NB), :
                ].astype(BF16)
            return carry

        lax.fori_loop(0, 2 * D // 128, gu, 0)

        def down(j, carry):
            at = pl.multiple_of(p.TG + j * 896, 128)
            stage[0:896, :] = tall[pl.ds(at, 896), :].astype(F32)
            row = pl.multiple_of(j * 128, 128)
            for s in range(7):
                wd[pl.ds(row, 128), 128 * s : 128 * s + 128] = stage[
                    pl.ds(s, 128, stride=7), :
                ].astype(BF16)
            return carry

        lax.fori_loop(0, p.NB, down, 0)

    return pl.pallas_call(
        kernel,
        name="load_mlp_weights",
        out_shape=(
            jax.ShapeDtypeStruct((2 * D, width), BF16),
            jax.ShapeDtypeStruct((width, D), BF16),
        ),
        in_specs=[sspec()] * 3 + [vspec()] * 2,
        out_specs=(vspec(),) * 2,
        scratch_shapes=[
            VM((p.TR + p.U, 128), BF16),
            VM((max(128 * p.NB, 896), 128), F32),
        ],
        compiler_params=params(),
        cost_estimate=cost(0, 40e6),
    )(scal, a_tab, n_tab, pieces, rel)


def mlp_grads(p, scal, a_tab, seconds, cots, hidden, d_gate, d_up):
    count = p.ctx * p.dp
    per = 128 * p.NB
    toks = seconds[0].shape[0]
    blocks = len(seconds)
    total_t = toks * blocks
    sizes = [up(s[4], 16) for s in p.wd_seg]
    total = max(sum(sizes), 16)
    half = 1
    rows = D // half
    steps_g = 2 * half
    slots = p.NB // 2 if p.NB % 2 == 0 else p.NB
    steps = steps_g + p.NB // slots

    def kernel(s_ref, a_ref, *refs):
        s_refs, c_refs = refs[:blocks], refs[blocks : 2 * blocks]
        h_ref, g_ref, u_ref, pieces, wdsp, tall, stage, sem = refs[2 * blocks :]
        d = s_ref[0]
        step = pl.program_id(0)

        @pl.when(step == 0)
        def _():
            tall[p.TR : p.TR + p.U, :] = jnp.zeros((p.U, 128), BF16)

        def columns(src):
            lhs = jnp.concatenate([r[...] for r in s_refs], axis=0) if blocks > 1 else s_refs[0][...]
            grad = dot_tn(lhs, src[...])
            size = rows * p.NB
            for s in range(p.NB):
                stage[pl.ds(s, rows, stride=p.NB), :] = grad[:, 128 * s : 128 * s + 128]
            at = pl.multiple_of(step * size, 128)
            tall[pl.ds(at, size), :] = stage[0:size, :].astype(BF16)

        @pl.when(step < half)
        def _():
            columns(g_ref)

        @pl.when(jnp.logical_and(step >= half, step < steps_g))
        def _():
            columns(u_ref)

        @pl.when(step >= steps_g)
        def _():
            rhs = jnp.concatenate([r[...] for r in c_refs], axis=0) if blocks > 1 else c_refs[0][...]
            grad = dot_tn(h_ref[...], rhs)
            size = slots * 896
            for s in range(7):
                stage[pl.ds(s, slots * 128, stride=7), :] = grad[:, 128 * s : 128 * s + 128]
            at = pl.multiple_of(p.TG + (step - steps_g) * size, 128)
            tall[pl.ds(at, size), :] = stage[0:size, :].astype(BF16)

        @pl.when(step == steps - 1)
        def _():
            def copy_of(j):
                at = pl.multiple_of(a_ref[j], 16)
                return pltpu.make_async_copy(tall.at[pl.ds(at, p.U), :], pieces.at[j], sem.at[j])

            def start(j, carry):
                copy_of(j).start()
                return carry

            def wait(j, carry):
                copy_of(j).wait()
                return carry

            lax.fori_loop(0, count, start, 0)
            wdsp[...] = jnp.zeros(wdsp.shape, BF16)
            pos = 0
            for (dest, t0, _, _, _), size in zip(p.wd_seg, sizes):

                @pl.when(d == dest)
                def _():
                    wdsp[pos : pos + size, :] = tall[t0 : t0 + size, :]

                pos += size
            lax.fori_loop(0, count, wait, 0)

    def s_map(i):
        return (0, jnp.where(i < steps_g, i % half, half - 1))

    def h_map(i):
        return (0, jnp.maximum(i - steps_g, 0))

    full = pl.BlockSpec((total_t, per), lambda i: (0, 0))
    return pl.pallas_call(
        kernel,
        name="mlp_grads",
        grid=(steps,),
        out_shape=(
            jax.ShapeDtypeStruct((count, p.U, 128), BF16),
            jax.ShapeDtypeStruct((total, 128), BF16),
        ),
        in_specs=[sspec(), sspec()]
        + [pl.BlockSpec((toks, rows), s_map)] * blocks
        + [pl.BlockSpec((toks, D), lambda i: (0, 0))] * blocks
        + [pl.BlockSpec((total_t, slots * 128), h_map), full, full],
        out_specs=(aspec(), pl.BlockSpec((total, 128), lambda i: (0, 0))),
        scratch_shapes=[
            VM((p.TR + p.U, 128), BF16),
            VM((max(rows * p.NB, slots * 896), 128), F32),
            pltpu.SemaphoreType.DMA((count,)),
        ],
        compiler_params=params(),
        cost_estimate=cost(6 * total_t * D * per, 30e6),
    )(scal, a_tab, *seconds, *cots, hidden, d_gate, d_up)


def dot(a, b):
    return jnp.dot(a, b, preferred_element_type=F32)


def dot_nt(a, b):
    return lax.dot_general(a, b, (((1,), (1,)), ((), ())), preferred_element_type=F32)


def dot_tn(a, b):
    return lax.dot_general(a, b, (((0,), (0,)), ((), ())), preferred_element_type=F32)


def blk(b):
    return slice(128 * b, 128 * b + 128)


def partner(u):
    lane = lax.broadcasted_iota(jnp.int32, u.shape, 1) % HEAD
    return jnp.where(lane < HEAD // 2, pltpu.roll(u, 128 - HEAD // 2, 1), pltpu.roll(u, HEAD // 2, 1))


def rms(values):
    return lax.rsqrt(jnp.sum(values * values, axis=1, keepdims=True) / D + RMS_EPS)


def attention_inputs(p, scal, mine, theirs, x, cosine, sine):
    toks, dp = x.shape[0], p.dp

    def kernel(s_ref, *refs):
        m_refs, t_refs = refs[:dp], refs[dp : 2 * dp]
        x_ref, c_ref, sn_ref, wqkv, wo, vec, n_ref, q_ref, kv_ref, rows, flat = refs[2 * dp :]
        d, core = s_ref[0], s_ref[1]
        for q in range(dp):
            rows[core, q] = m_refs[q][...]
            rows[1 - core, q] = t_refs[q][...]
        for f0, kk, dd, row0, length in p.att_seg:
            flat[f0 : f0 + length, :] = rows[kk, d ^ dd, row0 : row0 + length, :].astype(F32)
        for q in range(7):
            wqkv[:, blk(q)] = flat[pl.ds(q, D, stride=7), :].astype(BF16)
            wo[:, blk(q)] = flat[pl.ds(8073 + q, D, stride=7), :].astype(BF16)
        wqkv[:, 896:1024] = flat[6279 : 6279 + D, :].astype(BF16)
        wqkv[:, 1024:1152] = flat[7176 : 7176 + D, :].astype(BF16)
        vec[...] = jnp.zeros(vec.shape, F32)
        vec[0:7, :] = flat[6272:6279, :]
        vec[7:8, :] = flat[7175:7176, :]
        vec[8:9, :] = flat[8072:8073, :]
        for f0, kk, dd, row0, length in p.gain_seg:
            g = rows[kk, d ^ dd, row0 : row0 + up(length, 16), :].astype(F32)
            vec[9 + f0 - G0 : 9 + f0 - G0 + length, :] = g[0:length]
        xf = x_ref[...].astype(F32)
        scale = rms(xf)
        for b in range(7):
            n_ref[:, blk(b)] = (xf[:, blk(b)] * scale * vec[9 + b : 10 + b, :]).astype(BF16)
        qkv = dot(n_ref[...], wqkv[...])
        cs, sn = c_ref[...], sn_ref[...]

        def rotated(b):
            u = qkv[:, blk(b)] + vec[b : b + 1, :]
            return (u * cs + partner(u) * sn).astype(BF16)

        for b in range(7):
            q_ref[:, blk(b)] = (rotated(b).astype(F32) * HEAD**-0.5).astype(BF16)
        kv_ref[:, 0:128] = rotated(7)
        kv_ref[:, 128:256] = (qkv[:, blk(8)] + vec[8:9, :]).astype(BF16)

    return pl.pallas_call(
        kernel,
        name="attention_inputs",
        out_shape=(
            jax.ShapeDtypeStruct((D, 1152), BF16),
            jax.ShapeDtypeStruct((D, D), BF16),
            jax.ShapeDtypeStruct((24, 128), F32),
            jax.ShapeDtypeStruct((toks, D), BF16),
            jax.ShapeDtypeStruct((toks, D), BF16),
            jax.ShapeDtypeStruct((toks, 256), BF16),
        ),
        in_specs=[sspec()] + [vspec()] * (2 * dp + 3),
        out_specs=(vspec(),) * 6,
        scratch_shapes=[VM((2, dp, p.RA, 128), BF16), VM((ATT + 7, 128), F32)],
        compiler_params=params(),
        cost_estimate=cost(6e8, 12e6),
    )(scal, *mine, *theirs, x, cosine, sine)


def lane_low(shape):
    return lax.broadcasted_iota(jnp.int32, shape, len(shape) - 1) < HEAD


def half_variants(x, out, at):
    xf = x.astype(F32)
    rolled = pltpu.roll(xf, HEAD, 1)
    low = lane_low(xf.shape)
    out[0, at, :] = jnp.where(low, xf, 0.0).astype(BF16)
    out[1, at, :] = jnp.where(low, 0.0, rolled).astype(BF16)
    out[2, at, :] = jnp.where(low, rolled, 0.0).astype(BF16)
    out[3, at, :] = jnp.where(low, 0.0, xf).astype(BF16)


def half_variants_t(x, out, at):
    xf = x.astype(F32).T
    swapped = jnp.concatenate([xf[HEAD:], xf[:HEAD]], axis=0)
    low = lax.broadcasted_iota(jnp.int32, xf.shape, 0) < HEAD
    out[0, :, at] = jnp.where(low, xf, 0.0).astype(BF16)
    out[1, :, at] = jnp.where(low, 0.0, swapped).astype(BF16)
    out[2, :, at] = jnp.where(low, swapped, 0.0).astype(BF16)
    out[3, :, at] = jnp.where(low, 0.0, xf).astype(BF16)


def attention_forward(query, kvs, bias, x, w_out, vec):
    toks, length = query.shape[0], bias.shape[0]
    groups = HEADS // KV_HEADS
    count = len(kvs)

    def kernel(q_ref, *refs):
        kv_refs = refs[:count]
        b_ref, x_ref, w_ref, vec_ref, o_ref, l_ref, m_ref, s_ref, kvar, vvar, att = refs[count:]
        step = pl.program_id(0)

        @pl.when(step == 0)
        def _():
            for i, ref in enumerate(kv_refs):
                at = slice(i * toks, (i + 1) * toks)
                half_variants(ref[:, 0:128], kvar, at)
                half_variants_t(ref[:, 128:256], vvar, at)

        q_t = q_ref[...].astype(F32).T.astype(BF16)
        acc = None
        for half in range(2):
            var = 2 * ((2 * step + half) // groups) + half
            s = dot(kvar[var], q_t) + b_ref[...]
            peak = jnp.max(s, axis=0, keepdims=True)
            e = jnp.exp(s - peak)
            total = jnp.sum(e, axis=0, keepdims=True)
            part = dot(vvar[var], e.astype(BF16)) * (1.0 / total)
            acc = part if acc is None else acc + part
            l_ref[0, half : half + 1, :] = peak + jnp.log(total)
        out = acc.T
        o_ref[...] = out
        att[step] = out.astype(BF16)

        @pl.when(step == 6)
        def _():
            att_all = jnp.concatenate([att[b] for b in range(7)], axis=1)
            middle = x_ref[...].astype(F32) + dot(att_all, w_ref[...])
            m_ref[...] = middle
            scale = rms(middle)
            for b in range(7):
                s_ref[:, blk(b)] = (
                    middle[:, blk(b)] * scale * vec_ref[16 + b : 17 + b, :]
                ).astype(BF16)

    return pl.pallas_call(
        kernel,
        name="attention_forward",
        grid=(7,),
        out_shape=(
            jax.ShapeDtypeStruct((toks, D), F32),
            jax.ShapeDtypeStruct((7, 8, toks), F32),
            jax.ShapeDtypeStruct((toks, D), F32),
            jax.ShapeDtypeStruct((toks, D), BF16),
        ),
        in_specs=[pl.BlockSpec((toks, 128), lambda i: (0, i))] + [vspec()] * (count + 4),
        out_specs=(
            pl.BlockSpec((toks, 128), lambda i: (0, i)),
            pl.BlockSpec((1, 8, toks), lambda i: (i, 0, 0)),
            pl.BlockSpec((toks, D), lambda i: (0, 0)),
            pl.BlockSpec((toks, D), lambda i: (0, 0)),
        ),
        scratch_shapes=[
            VM((4, length, 128), BF16),
            VM((4, 128, length), BF16),
            VM((7, toks, 128), BF16),
        ],
        compiler_params=params(),
        cost_estimate=cost(8 * 14 * 256 * 2048 * 128, 8e6),
    )(query, *kvs, bias, x, w_out, vec)


def attention_backward(query, kvs, bias, lse, attended, middle, d_seconds, cot, w_out, vec):
    toks, length = query.shape[0], bias.shape[0]
    groups = HEADS // KV_HEADS
    count, extra = len(kvs), len(d_seconds)
    keep_rows = length // 2

    def kernel(q_ref, a_ref, l_ref, *refs):
        kv_refs, ds_refs = refs[:count], refs[count : count + extra]
        (
            b_ref, m_ref, c_ref, w_ref, vec_ref,
            dq_ref, keep_ref, give_ref, dm_ref, br_ref, g2_ref,
            kvar, ktvar, vvar, dk_acc, dv_acc, do_all,
        ) = refs[count + extra :]
        step = pl.program_id(0)

        @pl.when(step == 0)
        def _():
            for i, ref in enumerate(kv_refs):
                at = slice(i * toks, (i + 1) * toks)
                half_variants(ref[:, 0:128], kvar, at)
                half_variants(ref[:, 128:256], vvar, at)
                half_variants_t(ref[:, 0:128], ktvar, at)
            dk_acc[...] = jnp.zeros(dk_acc.shape, F32)
            dv_acc[...] = jnp.zeros(dv_acc.shape, F32)
            mid = m_ref[...]
            scale = rms(mid)
            unit = mid * scale
            grad = ds_refs[0][...]
            for ref in ds_refs[1:]:
                grad = grad + ref[...].astype(F32)
            both = grad * unit
            inner = jnp.zeros((toks, 1), F32)
            g2_ref[...] = jnp.zeros(g2_ref.shape, F32)
            for b in range(7):
                g2_ref[b : b + 1, :] = jnp.sum(both[:, blk(b)], axis=0, keepdims=True)
                inner = inner + jnp.sum(
                    both[:, blk(b)] * vec_ref[16 + b : 17 + b, :], axis=1, keepdims=True
                )
            inner = inner / D
            for b in range(7):
                dm = c_ref[:, blk(b)].astype(F32) + scale * (
                    grad[:, blk(b)] * vec_ref[16 + b : 17 + b, :] - unit[:, blk(b)] * inner
                )
                dm_ref[:, blk(b)] = dm
                br_ref[:, blk(b)] = dm.astype(BF16)
            d_out = dot_nt(br_ref[...], w_ref[...])
            for b in range(7):
                do_all[b] = d_out[:, blk(b)].astype(BF16)

        low = lane_low((toks, 128))
        q_f, do_f = q_ref[...].astype(F32), do_all[step].astype(F32)
        q_t, do_t = q_f.T.astype(BF16), do_f.T.astype(BF16)
        prod = (do_f * a_ref[...]).T
        acc = None
        for half in range(2):
            group = (2 * step + half) // groups
            var = 2 * group + half
            keep = low if half == 0 else jnp.logical_not(low)
            q_half = jnp.where(keep, q_f, 0.0).astype(BF16)
            do_half = jnp.where(keep, do_f, 0.0).astype(BF16)
            delta = jnp.sum(prod[HEAD * half : HEAD * half + HEAD], axis=0, keepdims=True)
            s = dot(kvar[var], q_t) + b_ref[...]
            prob = jnp.exp(s - l_ref[0, half : half + 1, :])
            dv_acc[group] += dot(prob.astype(BF16), do_half)
            dp = dot(vvar[var], do_t)
            ds = (prob * (dp - delta)).astype(BF16)
            dk_acc[group] += dot(ds, q_half)
            part = dot(ktvar[var], ds)
            acc = part if acc is None else acc + part
        dq_ref[...] = acc.T

        @pl.when(step == 6)
        def _():
            lowk = lane_low((length, 128))
            for i, a in enumerate((dk_acc, dv_acc)):
                one, two = a[0], a[1]
                one = one + pltpu.roll(one, HEAD, 1)
                two = two + pltpu.roll(two, HEAD, 1)
                res = jnp.where(lowk, one, two)
                keep_ref[:, blk(i)] = res[:keep_rows]
                give_ref[:, blk(i)] = res[keep_rows:].astype(BF16)

    def fixed(shape):
        return pl.BlockSpec(shape, lambda i: (0, 0))

    return pl.pallas_call(
        kernel,
        name="attention_backward",
        grid=(7,),
        out_shape=(
            jax.ShapeDtypeStruct((toks, D), F32),
            jax.ShapeDtypeStruct((keep_rows, 256), F32),
            jax.ShapeDtypeStruct((keep_rows, 256), BF16),
            jax.ShapeDtypeStruct((toks, D), F32),
            jax.ShapeDtypeStruct((toks, D), BF16),
            jax.ShapeDtypeStruct((8, 128), F32),
        ),
        in_specs=[
            pl.BlockSpec((toks, 128), lambda i: (0, i)),
            pl.BlockSpec((toks, 128), lambda i: (0, i)),
            pl.BlockSpec((1, 8, toks), lambda i: (i, 0, 0)),
        ]
        + [vspec()] * (count + extra + 5),
        out_specs=(
            pl.BlockSpec((toks, 128), lambda i: (0, i)),
            fixed((keep_rows, 256)),
            fixed((keep_rows, 256)),
            fixed((toks, D)),
            fixed((toks, D)),
            fixed((8, 128)),
        ),
        scratch_shapes=[
            VM((4, length, 128), BF16),
            VM((4, 128, length), BF16),
            VM((4, length, 128), BF16),
            VM((2, length, 128), F32),
            VM((2, length, 128), F32),
            VM((7, toks, 128), BF16),
        ],
        compiler_params=params(),
        cost_estimate=cost(20 * 14 * 256 * 2048 * 128, 12e6),
    )(query, attended, lse, *kvs, *d_seconds, bias, middle, cot, w_out, vec)


def attention_tail(p, scal, d_query, kv_grads, cosine, sine, normed, w_qkv, attended, branch, x, middle_grad, vec, g2):
    toks, dp, count = x.shape[0], p.dp, len(kv_grads)

    def kernel(s_ref, dq_ref, *refs):
        k_refs = refs[:count]
        (
            c_ref, sn_ref, n_ref, wq_ref, a_ref, b_ref, x_ref, m_ref, v_ref, g2_ref,
            in_ref, keep_ref, give_ref, dqkv, flat, rows, gains,
        ) = refs[count:]
        d, core = s_ref[0], s_ref[1]
        cs, sn = c_ref[...], sn_ref[...]

        def back(g):
            return (g * cs - partner(g) * sn).astype(BF16)

        kv = k_refs[0][...].astype(F32)
        for ref in k_refs[1:]:
            kv = kv + ref[...].astype(F32)
        for b in range(7):
            dqkv[:, blk(b)] = back(dq_ref[:, blk(b)] * HEAD**-0.5)
        dqkv[:, blk(7)] = back(kv[:, 0:128].astype(BF16).astype(F32))
        dqkv[:, blk(8)] = kv[:, 128:256].astype(BF16)
        g_all = dqkv[...]
        dw = dot_tn(n_ref[...], g_all)
        dwo = dot_tn(a_ref[...].astype(BF16), b_ref[...])
        sums = jnp.sum(g_all.astype(F32), axis=0, keepdims=True)
        for q in range(7):
            flat[pl.ds(q, D, stride=7), :] = dw[:, blk(q)]
            flat[pl.ds(8073 + q, D, stride=7), :] = dwo[:, blk(q)]
            flat[6272 + q : 6273 + q, :] = sums[:, blk(q)]
        flat[6279 : 6279 + D, :] = dw[:, 896:1024]
        flat[7176 : 7176 + D, :] = dw[:, 1024:1152]
        flat[7175:7176, :] = sums[:, blk(7)]
        flat[8072:8073, :] = sums[:, blk(8)]
        d_normed = dot_nt(g_all, wq_ref[...])
        xf = x_ref[...].astype(F32)
        scale = rms(xf)
        unit = xf * scale
        both = d_normed * unit
        inner = jnp.zeros((toks, 1), F32)
        gains[...] = jnp.zeros(gains.shape, F32)
        for b in range(7):
            gains[b : b + 1, :] = jnp.sum(both[:, blk(b)], axis=0, keepdims=True)
            gains[7 + b : 8 + b, :] = g2_ref[b : b + 1, :]
            inner = inner + jnp.sum(both[:, blk(b)] * v_ref[9 + b : 10 + b, :], axis=1, keepdims=True)
        inner = inner / D
        for b in range(7):
            in_ref[:, blk(b)] = m_ref[:, blk(b)] + scale * (
                d_normed[:, blk(b)] * v_ref[9 + b : 10 + b, :] - unit[:, blk(b)] * inner
            )
        rows[...] = jnp.zeros(rows.shape, BF16)
        for f0, kk, dd, row0, length in p.att_seg:
            rows[kk, dd, row0 : row0 + length, :] = flat[f0 : f0 + length, :].astype(BF16)
        for f0, kk, dd, row0, length in p.gain_seg:
            rows[kk, dd, row0 : row0 + length, :] = gains[f0 - G0 : f0 - G0 + length, :].astype(BF16)
        for q in range(dp):
            keep_ref[q] = rows[core, d ^ q]
            give_ref[q] = rows[1 - core, d ^ q]

    return pl.pallas_call(
        kernel,
        name="attention_tail",
        out_shape=(
            jax.ShapeDtypeStruct((toks, D), F32),
            jax.ShapeDtypeStruct((dp, p.RA, 128), BF16),
            jax.ShapeDtypeStruct((dp, p.RA, 128), BF16),
        ),
        in_specs=[sspec()] + [vspec()] * (count + 11),
        out_specs=(vspec(),) * 3,
        scratch_shapes=[
            VM((toks, 1152), BF16),
            VM((ATT + 7, 128), F32),
            VM((2, dp, p.RA, 128), BF16),
            VM((16, 128), F32),
        ],
        compiler_params=params(),
        cost_estimate=cost(2e9, 24e6),
    )(scal, d_query, *kv_grads, cosine, sine, normed, w_qkv, attended, branch, x, middle_grad, vec, g2)


def mlp_block(p, seconds, cots, w_gu, w_down):
    toks, count = seconds[0].shape[0], len(seconds)
    total = toks * count
    width = p.NB * 128
    step_w = 256 if p.NB % 2 == 0 else 128
    steps = width // step_w

    def kernel(*refs):
        s_refs, c_refs = refs[:count], refs[count : 2 * count]
        g_ref, u_ref, w_ref = refs[2 * count : 2 * count + 3]
        outs = refs[2 * count + 3 :]
        hid_ref, dg_ref, du_ref = outs[:3]
        ds_refs, y_refs = outs[3 : 3 + count], outs[3 + count : 3 + 2 * count]
        s_all, c_all, dsec, y = outs[3 + 2 * count :]
        j = pl.program_id(0)

        @pl.when(j == 0)
        def _():
            for i in range(count):
                s_all[i * toks : (i + 1) * toks, :] = s_refs[i][...]
                c_all[i * toks : (i + 1) * toks, :] = c_refs[i][...]

        gate = dot(s_all[...], g_ref[...])
        up_act = dot(s_all[...], u_ref[...])
        sig = jax.nn.sigmoid(gate)
        act = gate * sig
        hidden = (act * up_act).astype(BF16)
        d_hidden = dot_nt(c_all[...], w_ref[...])
        d_gate = (d_hidden * up_act * sig * (1.0 + gate * (1.0 - sig))).astype(BF16)
        d_up = (d_hidden * act).astype(BF16)
        hid_ref[...] = hidden
        dg_ref[...] = d_gate
        du_ref[...] = d_up

        @pl.when(j == 0)
        def _():
            dsec[...] = dot_nt(d_gate, g_ref[...]) + dot_nt(d_up, u_ref[...])
            y[...] = dot(hidden, w_ref[...])

        @pl.when(j > 0)
        def _():
            dsec[...] += dot_nt(d_gate, g_ref[...]) + dot_nt(d_up, u_ref[...])
            y[...] += dot(hidden, w_ref[...])

        @pl.when(j == steps - 1)
        def _():
            for i in range(count):
                at = slice(i * toks, (i + 1) * toks)
                ds_refs[i][...] = dsec[at, :].astype(ds_refs[i].dtype)
                y_refs[i][...] = y[at, :].astype(y_refs[i].dtype)

    wide = jax.ShapeDtypeStruct((total, width), BF16)
    narrow = [jax.ShapeDtypeStruct((toks, D), F32 if i == 0 else BF16) for i in range(count)]
    whole = pl.BlockSpec((toks, D), lambda j: (0, 0))
    piece = pl.BlockSpec((total, step_w), lambda j: (0, j))
    outs = pl.pallas_call(
        kernel,
        name="mlp_block",
        grid=(steps,),
        out_shape=(wide, wide, wide, *narrow, *narrow),
        in_specs=[whole] * (2 * count)
        + [
            pl.BlockSpec((D, step_w), lambda j: (0, j)),
            pl.BlockSpec((D, step_w), lambda j: (1, j)),
            pl.BlockSpec((step_w, D), lambda j: (j, 0)),
        ],
        out_specs=(piece, piece, piece) + (whole,) * (2 * count),
        scratch_shapes=[VM((total, D), BF16)] * 2 + [VM((total, D), F32)] * 2,
        compiler_params=params(),
        cost_estimate=cost(12 * total * D * width, 20e6),
    )(*seconds, *cots, w_gu, w_gu, w_down)
    return outs[:3], outs[3 : 3 + count], outs[3 + count :]


def adam_step(p, place, grad, lates, master, moment_one, moment_two, scale):
    n, dp = master.shape[0], p.dp
    size = 104
    full, rest = n // size, n % size
    low = n // 8 * 8

    def kernel(s_ref, g_ref, *refs):
        l_refs = refs[:dp]
        w_ref, m1_ref, m2_ref, wo_ref, o1_ref, o2_ref, acc = refs[dp:]
        d, first, each = s_ref[0], s_ref[1], s_ref[2]
        acc[0:n, :] = g_ref[...]
        for q in range(dp):
            base = first + (d ^ q) * each

            def add(j, carry):
                frm = pl.multiple_of(j * 16, 16)
                rows = l_refs[q][pl.ds(frm, 16), :].astype(F32)
                acc[pl.ds(base + frm, 16), :] = acc[pl.ds(base + frm, 16), :] + rows
                return carry

            lax.fori_loop(0, each // 16, add, 0)

        def update(at):
            g = acc[at, :] * scale
            one = BETA_ONE * m1_ref[at, :] + (1.0 - BETA_ONE) * g
            two = BETA_TWO * m2_ref[at, :] + (1.0 - BETA_TWO) * g * g
            w = w_ref[at, :]
            o1_ref[at, :] = one
            o2_ref[at, :] = two
            root = jnp.sqrt(two / (1.0 - BETA_TWO**STEP)) + ADAM_EPS
            wo_ref[at, :] = w - LEARN_RATE * (
                (one / (1.0 - BETA_ONE**STEP)) / root + DECAY_RATE * w
            )

        def loop(j, carry):
            update(pl.ds(pl.multiple_of(j * size, 8), size))
            return carry

        lax.fori_loop(0, full, loop, 0)
        if rest:
            update(slice(full * size, n))

    out = jax.ShapeDtypeStruct((n, 128), F32)
    return pl.pallas_call(
        kernel,
        name="adam_step",
        out_shape=(out, out, out),
        in_specs=[sspec()] + [vspec()] * (dp + 4),
        out_specs=(vspec(),) * 3,
        scratch_shapes=[VM((low + 8 + dp * p.nsm + 16, 128), F32)],
        compiler_params=params(),
        cost_estimate=cost(0, n * 4096),
    )(place, grad, *lates, master, moment_one, moment_two)


def rope_tables(positions):
    half_dim = HEAD // 2
    inverse = ROPE_BASE ** (-(jnp.arange(half_dim, dtype=F32) * 2.0 / HEAD))
    angles = positions.astype(F32)[:, None] * inverse[None, :]
    c, s = jnp.cos(angles), jnp.sin(angles)
    return jnp.concatenate([c, c, c, c], axis=1), jnp.concatenate([-s, s, -s, s], axis=1)


def ancestor_bits(parents):
    tree_count, seg_count = parents.shape
    current = jnp.broadcast_to(
        jnp.arange(seg_count, dtype=jnp.int32)[None, :], (tree_count, seg_count)
    )
    bits = jnp.zeros((tree_count, seg_count), jnp.int32)
    hot = jnp.arange(seg_count, dtype=jnp.int32)
    for _ in range(seg_count):
        bits = jnp.bitwise_or(bits, jnp.left_shift(jnp.ones_like(current), current))
        chosen = current[:, :, None] == hot[None, None, :]
        current = jnp.sum(jnp.where(chosen, parents[:, None, :], 0), axis=2)
    return bits


def swap(x, axis, size, mask):
    return lax.ppermute(x, axis, [(i, i ^ mask) for i in range(size)])


def dyn(x, i):
    return lax.dynamic_index_in_dim(x, i, 0, keepdims=False)


def mask_bias(c, toks, nz, parents, lengths):
    per_tree = TREE_LEN // toks
    tree = c // per_tree
    ends, bits = dyn(jnp.cumsum(lengths, axis=1), tree), dyn(ancestor_bits(parents), tree)

    def seg_of(index):
        return jnp.sum((index[:, None] >= ends[None, :]).astype(jnp.int32), axis=1)

    tok_iota = jnp.arange(toks, dtype=jnp.int32)
    q_idx = (c % per_tree) * toks + tok_iota
    k_idx = jnp.concatenate(
        [
            ((c ^ (2 * q) ^ r) % per_tree) * toks + tok_iota
            for r in range(2)
            for q in range(per_tree // 2)
        ]
    )
    q_seg, k_seg = seg_of(q_idx), seg_of(k_idx)
    seg_iota = jnp.arange(ends.shape[0], dtype=jnp.int32)
    q_bits = jnp.sum(jnp.where(q_seg[:, None] == seg_iota[None, :], bits[None, :], 0), axis=1)
    allowed = (jnp.right_shift(q_bits[None, :], k_seg[:, None]) & 1 == 1) & (
        k_idx[:, None] <= q_idx[None, :]
    )
    return jnp.where(allowed, 0.0, NEG_FILL).astype(F32)


def body(p, inputs, cotangent, parents, lengths, positions, master, moment_one, moment_two):
    toks = inputs.shape[0]
    dp, ctx, n, U, nz = p.dp, p.ctx, p.n, p.U, p.nz
    tz = TREE_LEN // toks // 2
    d, c = lax.axis_index("dp"), lax.axis_index("ctx")
    core, z = jnp.bitwise_and(c, 1), c // 2
    scal = jnp.stack([d, core]).astype(jnp.int32)
    owner = d * ctx + c

    def pick(table, i):
        return dyn(jnp.asarray(table), i)

    a_tab, n_tab = pick(p.aT, d), pick(p.nT, d)

    pieces = spread_rows(pick(p.fwd, owner), master).reshape(dp, U, 128)
    gathered = jnp.stack([pieces[0]] + [swap(pieces[q], "dp", dp, q) for q in range(1, dp)])
    special = jnp.concatenate([dyn(gathered, d ^ s)[U - p.nsA[s] :] for s in p.loA], axis=0)
    by_z = jnp.stack([special] + [swap(special, "ctx", ctx, 2 * q) for q in range(1, nz)])
    mine = [
        jnp.concatenate(
            [dyn(by_z, z ^ zz)[p.loA[s] : p.loA[s] + p.nsA[s]] for s, zz in p.pairs], axis=0
        )
    ]
    mine += [swap(mine[0], "dp", dp, q) for q in range(1, dp)]
    theirs = [swap(m, "ctx", ctx, 1) for m in mine]
    gathered, by_z = lax.optimization_barrier((gathered, by_z))
    mlp_pieces = lax.all_gather(gathered, "ctx", axis=0)
    bias = mask_bias(c, toks, nz, parents, lengths)
    cosine, sine = rope_tables(positions)
    cots = [cotangent] + [swap(cotangent, "dp", dp, q) for q in range(1, dp)]

    w_qkv, w_out, vec, normed, query, kv = attention_inputs(
        p, scal, mine, theirs, inputs, cosine, sine
    )
    kvs = [kv] + [swap(kv, "ctx", ctx, 2 * q) for q in range(1, tz)]
    kvs += [swap(k, "ctx", ctx, 1) for k in kvs]
    attended, lse, middle, second = attention_forward(query, kvs, bias, inputs, w_out, vec)

    if p.ownB:
        ds, cb = p.ownB[0]
        rows_b = dyn(mlp_pieces[cb], d ^ ds)[U - p.nsB[ds] :]
    else:
        rows_b = jnp.zeros((p.RB, 128), BF16)
    rel_b = jnp.stack([rows_b] + [swap(rows_b, "dp", dp, q) for q in range(1, dp)])
    w_gu, w_down = load_mlp_weights(
        p, scal, a_tab, n_tab, mlp_pieces.reshape(ctx * dp, U, 128), rel_b
    )
    seconds = [second] + [swap(second, "dp", dp, q) for q in range(1, dp)]
    kept, d_parts, y_parts = mlp_block(p, seconds, cots, w_gu, w_down)
    d_seconds = [d_parts[0]] + [swap(d_parts[q], "dp", dp, q) for q in range(1, dp)]
    grad_pieces, wd_rows = mlp_grads(p, scal, a_tab, seconds, cots, *kept)
    own_pieces = lax.psum_scatter(
        grad_pieces.reshape(ctx, dp, U, 128), "ctx", scatter_dimension=0, tiled=False
    )
    activations = middle + y_parts[0]
    for q in range(1, dp):
        activations = activations + swap(y_parts[q], "dp", dp, q).astype(F32)
    activations = activations.astype(BF16)

    chunks = [[] for _ in range(dp)]
    pos = 0
    for _, _, dd, row0, length in p.wd_seg:
        chunks[dd].append(wd_rows[pos : pos + length])
        pos += up(length, 16)
    chunks = jnp.stack(
        [
            jnp.pad(
                jnp.concatenate(ch, axis=0) if ch else jnp.zeros((0, 128), BF16),
                ((0, p.RB - sum(x.shape[0] for x in ch)), (0, 0)),
            )
            for ch in chunks
        ]
    )
    late_b = dyn(chunks, d).astype(F32)
    for q in range(1, dp):
        late_b = late_b + swap(dyn(chunks, d ^ q), "dp", dp, q).astype(F32)
    late_b = late_b.astype(BF16)
    give_b = swap(late_b, "ctx", ctx, 1)

    d_query, d_kv, d_kv_give, middle_grad, branch, gain_two = attention_backward(
        query, kvs, bias, lse, attended, middle, d_seconds, cotangent, w_out, vec
    )
    d_kv = (d_kv + swap(d_kv_give, "ctx", ctx, 1).astype(F32)).reshape(tz, toks, 256)
    kv_grads = [d_kv[0]] + [swap(d_kv[q].astype(BF16), "ctx", ctx, 2 * q) for q in range(1, tz)]
    input_grad, keep, give = attention_tail(
        p, scal, d_query, kv_grads, cosine, sine, normed, w_qkv, attended, branch, inputs,
        middle_grad, vec, gain_two,
    )

    pair = (keep.astype(F32) + swap(give, "ctx", ctx, 1).astype(F32)).astype(BF16)
    chunk = pair[0].astype(F32)
    for q in range(1, dp):
        chunk = chunk + swap(pair[q], "dp", dp, q).astype(F32)
    chunk = chunk.astype(BF16)
    late_b = (late_b.astype(F32) + give_b.astype(F32)).astype(BF16)
    messages = []
    for parts in p.msg:
        rows = [(chunk if kind == "A" else late_b)[off : off + ln] for kind, off, ln in parts]
        short = p.M - sum(ln for _, _, ln in parts)
        messages.append(jnp.concatenate(rows + [jnp.zeros((short, 128), BF16)], axis=0))
    messages = jnp.stack(messages)
    late = dyn(messages, z).astype(F32)
    for q in range(1, nz):
        late = late + swap(dyn(messages, z ^ q), "ctx", ctx, 2 * q).astype(F32)
    late = jnp.pad(late.astype(BF16), ((0, p.nsm), (0, 0)))
    starts = pick(p.offM, z)

    def late_for(q):
        return lax.dynamic_slice_in_dim(late, dyn(starts, d ^ q), p.nsm, 0)

    lates = [late_for(0)] + [swap(late_for(q), "dp", dp, q) for q in range(1, dp)]

    parts = [own_pieces[0]] + [swap(own_pieces[q], "dp", dp, q) for q in range(1, dp)]
    grad = collect_rows(pick(p.back, owner), parts, n)
    place = jnp.concatenate([d.reshape(1).astype(jnp.int32), pick(p.late, owner)])
    new_master, new_one, new_two = adam_step(
        p, place, grad, lates, master, moment_one, moment_two, float(toks * dp * ctx) ** -0.5
    )
    return (activations, input_grad, new_master, new_one, new_two)


def solution(mesh):
    dp, ctx = mesh.shape["dp"], mesh.shape["ctx"]

    def run(inputs, cotangent, parents, lengths, positions, master, moment_one, moment_two):
        p = make(dp, ctx, master.shape[0] // (dp * ctx))
        row = P(("dp", "ctx"), None)
        step = jax.shard_map(
            functools.partial(body, p),
            mesh=mesh,
            in_specs=(row, row, P("dp", None), P("dp", None), P(("dp", "ctx")), row, row, row),
            out_specs=(row,) * 5,
            check_vma=False,
        )
        return step(
            inputs, cotangent, parents, lengths, positions, master, moment_one, moment_two
        )

    return run
```
